32 devices in a mesh: dp: 8 (over z, y), fsdp: 4 (over x, core).
Axes of the slice: x: 2, y: 2, z: 4, core: 2. Of those that a mesh axis runs over, the one named last changes fastest.
Arguments:
- hidden_in: float32 [8192, 768], P(('dp', 'fsdp')), may hold values from -6 to 6
- cotangent: float32 [8192, 768], P(('dp', 'fsdp')), may hold values from -6 to 6
- seq_ids: int32 [8192], P(('dp', 'fsdp')), may hold values from -1 to 8191, as said below
- norm_gain: bfloat16 [768], P(('dp', 'fsdp')), may hold values from 0.5 to 1.5
- in_weight: bfloat16 [768, 3352], P(('dp', 'fsdp')), may hold values from -0.21875 to 0.21875
- conv_weight: bfloat16 [4, 1792], P(None, ('dp', 'fsdp')), may hold values from -3 to 3
- conv_bias: bfloat16 [1792], P(('dp', 'fsdp')), may hold values from -3 to 3
- out_gain: bfloat16 [1536], P(('dp', 'fsdp')), may hold values from 0.5 to 1.5
- out_weight: bfloat16 [1536, 768], P(('dp', 'fsdp')), may hold values from -0.15625 to 0.15625
- decay_log: float32 [24], replicated, may hold values from 0 to 2.77
- skip_gain: float32 [24], replicated, may hold values from 0.5 to 1.5
- step_bias: float32 [24], replicated, may hold values from -4.6 to -0.5
Outputs:
- block_out: float32 [8192, 768], P(('dp', 'fsdp'))
- grad_hidden: float32 [8192, 768], P(('dp', 'fsdp'))
- grad_norm_gain: float32 [768], P(('dp', 'fsdp'))
- grad_in_weight: float32 [768, 3352], P(('dp', 'fsdp'))
- grad_conv_weight: float32 [4, 1792], P(None, ('dp', 'fsdp'))
- grad_conv_bias: float32 [1792], P(('dp', 'fsdp'))
- grad_out_gain: float32 [1536], P(('dp', 'fsdp'))
- grad_out_weight: float32 [1536, 768], P(('dp', 'fsdp'))
- grad_decay_log: float32 [24], replicated
- grad_skip_gain: float32 [24], replicated
- grad_step_bias: float32 [24], replicated
The draws below stay inside these ranges and needn't reach their ends.
Inputs may be any that keep to these rules, and one draw needn't show every extreme that they name: `seq_ids`: in each aligned block of 256 slots the live slots come first and the rest hold -1; a sequence fills consecutive slots inside one block and its numbers rise along the slots; a sequence has at most 256 tokens, and some sequence has exactly 256; the first block has no empty slot.
All inputs are finite; a program needn't handle non-finite values.
Results may differ from the reference program's by a relative error of at most 0.015.
Values may be sent and summed in bfloat16 or wider, within the bound.
A program may use at most 128 MiB of HBM per device.

```python
from functools import partial
import jax
import jax.numpy as jnp
from jax import lax

D = 768
NS = 128
HD = 64
NH = 24
KC = 4
SPAN = 128
SEQ_MAX = 256
TOK_DEV = 256
DI = 1536
CONV = 1792
DIN = 3352
TOKENS = 8192


def draw_seq_ids(key, part):
    groups = TOKENS // TOK_DEV
    count_key, start_key = jax.random.split(jax.random.fold_in(key, 7))
    counts = jax.random.randint(count_key, (groups,), TOK_DEV // 4, TOK_DEV + 1)
    counts = jnp.where(jnp.arange(groups) == 0, TOK_DEV, counts)
    slots = jnp.arange(TOK_DEV)[None, :]
    group_row = jnp.arange(groups)[:, None]
    starts = jax.random.randint(start_key, (groups, TOK_DEV), 0, 96) == 0
    starts = starts | (slots % SEQ_MAX == 0)
    starts = starts & ~((group_row == 0) & (slots % SEQ_MAX != 0))
    number = jnp.cumsum(starts.astype(jnp.int32), axis=1) - 1 + group_row * TOK_DEV
    return jnp.where(slots < counts[:, None], number, -1).reshape(-1).astype(jnp.int32)


def levels(key, dims, cuts, smallest, high):
    def one(axis_at, parts):
        draws = jax.random.uniform(jax.random.fold_in(jax.random.fold_in(key, 6), axis_at), (parts,), jnp.float32, smallest / len(cuts), high / len(cuts))
        return jnp.repeat(jnp.exp(draws), dims[axis_at] // parts).reshape((-1,) + (1,) * (len(dims) - axis_at - 1))

    loudness = one(*cuts[0])
    for cut in cuts[1:]:
        loudness = loudness * one(*cut)
    return loudness


def gaussian(key, shape, deviation, bound, shards=(), held_as=jnp.bfloat16):
    values = jax.random.normal(key, shape, jnp.float32) * deviation
    if len(shards) > 0:
        values = levels(key, shape, shards, -0.22, 0.18) * values
    return jnp.clip(values, min=-bound, max=bound).astype(held_as)


def setup_inputs(seed: int = 0) -> dict:
    streams_of = jax.random.split(jax.random.key(seed), 13)
    hidden_in = gaussian(streams_of[0], (TOKENS, D), 1.0, 6.0, ((0, 32),), jnp.float32)
    cotangent = gaussian(streams_of[1], (TOKENS, D), 1.0, 6.0, ((0, 32),), jnp.float32)
    seq_ids = draw_seq_ids(jax.random.fold_in(streams_of[12], 71), 0)
    norm_gain = jnp.clip(1.0 + 0.1 * jax.random.normal(streams_of[3], (D,), jnp.float32), 0.5, 1.5).astype(jnp.bfloat16)
    in_weight = gaussian(streams_of[4], (D, DIN), D ** -0.5, 0.21875, ((0, 32),))
    conv_weight = gaussian(streams_of[5], (KC, CONV), KC ** -0.5, 3.0, ((1, 32),))
    conv_bias = gaussian(streams_of[6], (CONV,), 0.5, 3.0, ((0, 32),))
    out_gain = jnp.clip(1.0 + 0.1 * jax.random.normal(streams_of[7], (DI,), jnp.float32), 0.5, 1.5).astype(jnp.bfloat16)
    out_weight = gaussian(streams_of[8], (DI, D), DI ** -0.5, 0.15625, ((0, 32),))
    decay_log = jnp.clip(jax.random.uniform(streams_of[9], (NH,), jnp.float32, 0.0, 2.77), 0.0, 2.77)
    skip_gain = jnp.clip(jax.random.uniform(streams_of[10], (NH,), jnp.float32, 0.5, 1.5), 0.5, 1.5)
    step_bias = jnp.clip(jax.random.uniform(streams_of[11], (NH,), jnp.float32, -4.6, -0.5), -4.6, -0.5)
    return dict(hidden_in=hidden_in, cotangent=cotangent, seq_ids=seq_ids, norm_gain=norm_gain, in_weight=in_weight, conv_weight=conv_weight, conv_bias=conv_bias, out_gain=out_gain, out_weight=out_weight, decay_log=decay_log, skip_gain=skip_gain, step_bias=step_bias)


EPS = 1e-05

def norm_input(hidden, gain):
    scale = lax.rsqrt(lax.optimization_barrier(jnp.mean(hidden * hidden, axis=-1, keepdims=True)) + EPS)
    return hidden * scale * gain[None, :]

def mixer(projected, conv_kernel, conv_shift, out_scale, decay_log, skip_gain, step_bias, seq_index):
    length = projected.shape[0]
    gate_part = projected[:, :DI]
    conv_in = projected[:, DI:DI + CONV]
    step_raw = projected[:, DI + CONV:]
    live_rows = (seq_index >= 0).astype(jnp.float32)
    summed = conv_shift[None, :] + conv_in * conv_kernel[KC - 1][None, :]
    for offset in range(1, KC):
        earlier = jnp.concatenate([jnp.zeros((offset, CONV), jnp.float32), conv_in[:length - offset]], axis=0)
        matched = (seq_index[offset:] == seq_index[:length - offset]).astype(jnp.float32)
        same_seq = jnp.concatenate([jnp.zeros((offset,), jnp.float32), matched], axis=0)
        summed = summed + earlier * same_seq[:, None] * conv_kernel[KC - 1 - offset][None, :]
    activated = jax.nn.silu(summed)
    values = activated[:, :DI]
    in_state = activated[:, DI:DI + NS]
    out_state = activated[:, DI + NS:]
    step_size = jax.nn.softplus(step_raw + step_bias[None, :])
    log_decay = step_size * (-jnp.exp(decay_log))[None, :]
    blocks = length // SPAN
    scaled = (values.reshape(length, NH, HD) * step_size[:, :, None]).reshape(blocks, SPAN, NH, HD)
    keys_in = in_state.reshape(blocks, SPAN, NS)
    query_out = out_state.reshape(blocks, SPAN, NS)
    seq_blocks = seq_index.reshape(blocks, SPAN)
    running = jnp.cumsum(log_decay.reshape(blocks, SPAN, NH), axis=1).transpose(0, 2, 1)
    row_pos = lax.broadcasted_iota(jnp.int32, (SPAN, SPAN), 0)
    col_pos = lax.broadcasted_iota(jnp.int32, (SPAN, SPAN), 1)
    causal = (row_pos >= col_pos).astype(jnp.float32)
    pair_mask = (seq_blocks[:, :, None] == seq_blocks[:, None, :]).astype(jnp.float32) * causal[None]
    intersection = jnp.einsum('cqn,csn->cqs', query_out, keys_in, precision=lax.Precision.HIGHEST)
    gaps = running[:, :, :, None] - running[:, :, None, :]
    decays = jnp.exp(gaps * pair_mask[:, None]) * pair_mask[:, None]
    mixing = decays * intersection[:, None]
    inner_out = jnp.einsum('chqs,cshp->cqhp', mixing, scaled, precision=lax.Precision.HIGHEST)
    last_seq = seq_blocks[:, -1]
    end_total = running[:, :, -1]
    tail_mask = (seq_blocks == last_seq[:, None]).astype(jnp.float32)
    to_end = jnp.exp((end_total[:, :, None] - running) * tail_mask[:, None]) * tail_mask[:, None]
    block_state = jnp.einsum('csn,chs,cshp->chnp', keys_in, to_end, scaled, precision=lax.Precision.HIGHEST)
    prior_seq = jnp.concatenate([jnp.full((1,), -2, jnp.int32), last_seq[:-1].astype(jnp.int32)])
    carried = (last_seq == prior_seq).astype(jnp.float32)

    def advance(state, inputs):
        fresh, factor, flag = inputs
        return (state * factor[:, None, None] * flag + fresh, state)
    _, incoming = lax.scan(advance, jnp.zeros((NH, NS, HD), jnp.float32), (block_state, jnp.exp(end_total), carried))
    entering = (seq_blocks == prior_seq[:, None]).astype(jnp.float32)
    from_state = jnp.einsum('cqn,chnp->cqhp', query_out, incoming, precision=lax.Precision.HIGHEST)
    growth = jnp.exp(running).transpose(0, 2, 1) * entering[:, :, None]
    result = (inner_out + from_state * growth[:, :, :, None]).reshape(length, NH, HD)
    result = result + skip_gain[None, :, None] * values.reshape(length, NH, HD)
    gated = result.reshape(length, DI) * jax.nn.silu(gate_part)
    scale = lax.rsqrt(lax.optimization_barrier(jnp.mean(gated * gated, axis=-1, keepdims=True)) + EPS)
    return gated * scale * out_scale[None, :] * live_rows[:, None]

def rounded(value):
    return lax.optimization_barrier(value.astype(jnp.bfloat16)).astype(jnp.float32)

def reference(hidden_in, cotangent, seq_ids, norm_gain, in_weight, conv_weight, conv_bias, out_gain, out_weight, decay_log, skip_gain, step_bias):
    groups = TOKENS // TOK_DEV
    gain_in = norm_gain.astype(jnp.float32)
    kernel = conv_weight.astype(jnp.float32)
    shift = conv_bias.astype(jnp.float32)
    gain_out = out_gain.astype(jnp.float32)
    contract_rows = (((0,), (0,)), ((), ()))
    contract_cols = (((1,), (1,)), ((), ()))

    def one_block(totals, inputs):
        hidden, upstream, seq_index = inputs
        normed, norm_pull = jax.vjp(norm_input, hidden, gain_in)
        normed_b = normed.astype(jnp.bfloat16)
        projected = jnp.dot(normed_b, in_weight, preferred_element_type=jnp.float32)
        mixed_out, mix_pull = jax.vjp(partial(mixer, seq_index=seq_index), projected, kernel, shift, gain_out, decay_log, skip_gain, step_bias)
        mixed_b = mixed_out.astype(jnp.bfloat16)
        output = hidden + jnp.dot(mixed_b, out_weight, preferred_element_type=jnp.float32)
        upstream_b = upstream.astype(jnp.bfloat16)
        grad_wout = lax.dot_general(mixed_b, upstream_b, contract_rows, preferred_element_type=jnp.float32)
        d_mixed = lax.dot_general(upstream_b, out_weight, contract_cols, preferred_element_type=jnp.float32)
        pulled = mix_pull(d_mixed)
        d_proj_b = pulled[0].astype(jnp.bfloat16)
        grad_win = lax.dot_general(normed_b, d_proj_b, contract_rows, preferred_element_type=jnp.float32)
        d_normed = lax.dot_general(d_proj_b, in_weight, contract_cols, preferred_element_type=jnp.float32)
        d_hidden, grad_gain = norm_pull(d_normed)
        new_totals = (totals[0] + rounded(grad_gain), totals[1] + rounded(grad_win), totals[2] + rounded(pulled[1]), totals[3] + rounded(pulled[2]), totals[4] + rounded(pulled[3]), totals[5] + rounded(grad_wout), totals[6] + pulled[4], totals[7] + pulled[5], totals[8] + pulled[6])
        return (new_totals, (output, upstream + d_hidden))
    start = (jnp.zeros((D,), jnp.float32), jnp.zeros((D, DIN), jnp.float32), jnp.zeros((KC, CONV), jnp.float32), jnp.zeros((CONV,), jnp.float32), jnp.zeros((DI,), jnp.float32), jnp.zeros((DI, D), jnp.float32), jnp.zeros((NH,), jnp.float32), jnp.zeros((NH,), jnp.float32), jnp.zeros((NH,), jnp.float32))
    totals, outputs = lax.scan(one_block, start, (hidden_in.reshape(groups, TOK_DEV, D), cotangent.reshape(groups, TOK_DEV, D), seq_ids.reshape(groups, TOK_DEV)))
    return (outputs[0].reshape(TOKENS, D), outputs[1].reshape(TOKENS, D), totals[0], totals[1], totals[2], totals[3], totals[4], totals[5], totals[6], totals[7], totals[8])
```

```python
import jax
import jax.numpy as jnp
from jax import lax
from jax.experimental import pallas as pl
from jax.experimental.pallas import tpu as pltpu
from jax.sharding import PartitionSpec as P

NS = 128
HD = 64
NH = 24
KC = 4
DI = 1536
CONV = 1792
LANE = 128
EPS = 1e-05
AXES = ("dp", "fsdp")
F32 = jnp.float32
BF16 = jnp.bfloat16
HIGH = lax.Precision.HIGHEST
VM = pl.BlockSpec(memory_space=pltpu.VMEM)


def sds(*shape, dtype=F32):
    return jax.ShapeDtypeStruct(shape, dtype)


def cols(k, width=LANE):
    return pl.ds(pl.multiple_of(k * width, LANE), width)


def sigmoid(x):
    return 1.0 / (1.0 + jnp.exp(-x))


def dot(a, b, dims=((1,), (0,)), precision=None):
    return lax.dot_general(
        a, b, (dims, ((), ())), precision=precision, preferred_element_type=F32
    )


def pair_masks():
    lane = lax.broadcasted_iota(jnp.int32, (1, LANE), 1)
    first = (lane < HD).astype(F32)
    return first, 1.0 - first


def spread(width_from, k):
    head = lax.broadcasted_iota(jnp.int32, (width_from, LANE), 0)
    lane = lax.broadcasted_iota(jnp.int32, (width_from, LANE), 1)
    return (head == 2 * k + lane // HD).astype(F32)


def pair_decay(cum_e, cum_t, k, mask):
    two = cum_e[:, cols(k)]
    low = jnp.float32(-1e30)
    first = two[:, 0:1] - cum_t[pl.ds(2 * k, 1), :]
    second = two[:, HD : HD + 1] - cum_t[pl.ds(2 * k + 1, 1), :]
    return jnp.exp(jnp.where(mask, first, low)), jnp.exp(jnp.where(mask, second, low))


def same_mask(seq_col, seq_row):
    n = seq_col.shape[0]
    row = lax.broadcasted_iota(jnp.int32, (n, n), 0)
    col = lax.broadcasted_iota(jnp.int32, (n, n), 1)
    return (seq_col[...] == seq_row[...]) & (row >= col)


def forward_kernel(
    hidden, w_in, gain, taps, out_gain, skip_e, heads, meta, seq_col, seq_row,
    normed_b, proj, act, d_act, inner, mixed_b, gated, stats, step, step_e, cum_e, cum_t, scores,
):
    h = hidden[...]
    n, d = h.shape
    root = lax.rsqrt(jnp.sum(h * h, axis=-1, keepdims=True) / d + EPS)
    nb = (h * root * gain[...]).astype(BF16)
    normed_b[...] = nb
    wide = 3 * LANE

    @pl.loop(0, proj.shape[1] // wide)
    def _(k):
        proj[:, cols(k, wide)] = dot(nb, w_in[:, cols(k, wide)])

    same = [meta[:, j : j + 1] for j in range(KC - 1)]

    @pl.loop(0, CONV // LANE)
    def _(k):
        x = proj[:, cols(k + DI // LANE)]
        tap = taps[:, cols(k)]
        total = tap[KC : KC + 1] + x * tap[KC - 1 : KC]
        for j in range(1, KC):
            total = total + pltpu.roll(x, j, 0) * same[j - 1] * tap[KC - 1 - j : KC - j]
        sg = sigmoid(total)
        act[:, cols(k)] = total * sg
        d_act[:, cols(k)] = sg * (1.0 + total * (1.0 - sg))

    mask = same_mask(seq_col, seq_row)
    raw = proj[:, DI + CONV : DI + CONV + LANE] + heads[0:1]
    lane = lax.broadcasted_iota(jnp.int32, (1, LANE), 1)
    size = jnp.where(
        lane < NH, jnp.maximum(raw, 0.0) + jnp.log1p(jnp.exp(-jnp.abs(raw))), 0.0
    )
    step[...] = size
    running = dot(mask.astype(F32), size * heads[1:2], precision=HIGH)
    cum_t[...] = running.T
    b = act[:, DI : DI + NS].astype(BF16)
    c = act[:, DI + NS : DI + 2 * NS].astype(BF16)
    scores[...] = dot(c, b, ((1,), (1,)))
    first, second = pair_masks()
    stats[...] = jnp.zeros_like(stats)

    @pl.loop(0, NH // 2)
    def _(k):
        e = spread(LANE, k)
        cum_e[:, cols(k)] = dot(running, e, precision=HIGH)
        size_e = dot(size, e, precision=HIGH)
        step_e[:, cols(k)] = size_e
        decay0, decay1 = pair_decay(cum_e, cum_t, k, mask)
        v = act[:, cols(k)]
        x = v * size_e
        s = scores[...]
        y = dot((s * decay0).astype(BF16), (x * first).astype(BF16)) + dot(
            (s * decay1).astype(BF16), (x * second).astype(BF16)
        )
        inner[:, cols(k)] = y
        g = proj[:, cols(k)]
        z = (y + skip_e[:, cols(k)] * v) * g * sigmoid(g)
        gated[:, cols(k)] = z
        stats[...] += z * z

    scale = lax.rsqrt(jnp.sum(stats[...], axis=-1, keepdims=True) / DI + EPS)
    live = meta[:, KC - 1 : KC]
    stats[...] = jnp.where(lane < HD, scale, root)
    factor = scale * live

    @pl.loop(0, NH // 2)
    def _(k):
        mixed_b[:, cols(k)] = (gated[:, cols(k)] * factor * out_gain[:, cols(k)]).astype(BF16)


def backward_kernel(
    hidden, upstream, w_in, w_out, gain, taps, out_gain, skip_e, heads, meta, seq_col, seq_row,
    proj, act, d_act, inner, gated, stats, step, step_e, cum_e, cum_t, scores,
    grad_hidden, d_proj_b, g_gain, g_taps, g_out, g_heads,
    d_val, d_gated, acc, d_scores,
):
    h = hidden[...]
    n, d = h.shape
    up = upstream[...].astype(BF16)
    mask = same_mask(seq_col, seq_row)
    live = meta[:, KC - 1 : KC]
    scale = stats[:, 0:1]
    root = stats[:, HD : HD + 1]
    first, second = pair_masks()
    acc[...] = jnp.zeros_like(acc)

    @pl.loop(0, NH // 2)
    def _(k):
        dm = dot(up, w_out[cols(k), :], ((1,), (1,))) * live
        z = gated[:, cols(k)]
        g_out[:, cols(k)] = jnp.sum(dm * z * scale, axis=0, keepdims=True)
        u = dm * out_gain[:, cols(k)]
        d_gated[:, cols(k)] = u
        acc[...] += u * z

    pull = jnp.sum(acc[...], axis=-1, keepdims=True) * (scale * scale * scale) / DI
    d_scores[...] = jnp.zeros_like(d_scores)
    g_heads[...] = jnp.zeros_like(g_heads)
    tall = lax.broadcasted_iota(jnp.int32, (8, 1), 0)

    def body(k, carry):
        d_cum, d_step = carry
        e = spread(LANE, k)
        dz = scale * d_gated[:, cols(k)] - gated[:, cols(k)] * pull
        g = proj[:, cols(k)]
        sg = sigmoid(g)
        v = act[:, cols(k)]
        y = inner[:, cols(k)]
        skip = skip_e[:, cols(k)]
        d_proj_b[:, cols(k)] = (
            dz * (y + skip * v) * sg * (1.0 + g * (1.0 - sg))
        ).astype(BF16)
        dy = dz * g * sg
        size_e = step_e[:, cols(k)]
        x = (v * size_e).astype(BF16)
        dyb = dy.astype(BF16)
        dy0 = (dy * first).astype(BF16)
        dy1 = (dy * second).astype(BF16)
        decay0, decay1 = pair_decay(cum_e, cum_t, k, mask)
        s = scores[...]
        dx = dot((s * decay0).astype(BF16), dy0, ((0,), (0,))) + dot(
            (s * decay1).astype(BF16), dy1, ((0,), (0,))
        )
        d_scores[...] += dot(dy0, x, ((1,), (1,))) * decay0 + dot(dy1, x, ((1,), (1,))) * decay1
        d_val[:, cols(k)] = dx * size_e + skip * dy
        flow = dyb.astype(F32) * y - x.astype(F32) * dx
        d_cum = d_cum + dot(flow, e, ((1,), (1,)), precision=HIGH)
        d_step = d_step + dot(dx * v, e, ((1,), (1,)), precision=HIGH)
        skips = jnp.sum(dy * v, axis=0, keepdims=True)
        g_heads[...] += jnp.where(
            tall == 1, dot(jnp.broadcast_to(skips, (8, LANE)), e, ((1,), (1,)), precision=HIGH), 0.0
        )
        return d_cum, d_step

    zero = jnp.zeros((n, LANE), F32)
    d_cum, d_step = lax.fori_loop(0, NH // 2, body, (zero, zero))
    d_rate = dot(mask.astype(F32), d_cum, ((0,), (0,)), precision=HIGH)
    neg = heads[1:2]
    size = step[...]
    raw = proj[:, DI + CONV : DI + CONV + LANE] + heads[0:1]
    lane = lax.broadcasted_iota(jnp.int32, (1, LANE), 1)
    d_raw = jnp.where(lane < NH, (d_step + d_rate * neg) * sigmoid(raw), 0.0)
    d_proj_b[:, DI + CONV : DI + CONV + LANE] = d_raw.astype(BF16)
    g_decay = jnp.sum(d_rate * size * neg, axis=0, keepdims=True)
    g_step = jnp.sum(d_raw, axis=0, keepdims=True)
    g_heads[...] += jnp.where(tall == 0, g_decay, 0.0) + jnp.where(tall == 2, g_step, 0.0)

    b = act[:, DI : DI + NS].astype(BF16)
    c = act[:, DI + NS : DI + 2 * NS].astype(BF16)
    ds = d_scores[...].astype(BF16)
    d_val[:, DI : DI + NS] = dot(ds, c, ((0,), (0,)))
    d_val[:, DI + NS : DI + 2 * NS] = dot(ds, b)
    same = [meta[:, j : j + 1] for j in range(KC - 1)]

    @pl.loop(0, CONV // LANE)
    def _(k):
        x = proj[:, cols(k + DI // LANE)]
        tap = taps[:, cols(k)]
        dt = d_val[:, cols(k)] * d_act[:, cols(k)]
        g_taps[pl.ds(KC, 1), cols(k)] = jnp.sum(dt, axis=0, keepdims=True)
        g_taps[pl.ds(KC - 1, 1), cols(k)] = jnp.sum(dt * x, axis=0, keepdims=True)
        dc = dt * tap[KC - 1 : KC]
        for j in range(1, KC):
            ds_j = dt * same[j - 1]
            g_taps[pl.ds(KC - 1 - j, 1), cols(k)] = jnp.sum(
                ds_j * pltpu.roll(x, j, 0), axis=0, keepdims=True
            )
            dc = dc + pltpu.roll(ds_j, n - j, 0) * tap[KC - 1 - j : KC - j]
        d_proj_b[:, cols(k + DI // LANE)] = dc.astype(BF16)

    wide = 3 * LANE

    def add(k, total):
        return total + dot(d_proj_b[:, cols(k, wide)], w_in[:, cols(k, wide)], ((1,), (1,)))

    d_normed = lax.fori_loop(0, d_proj_b.shape[1] // wide, add, jnp.zeros((n, d), F32))
    g_gain[...] = jnp.sum(d_normed * h * root, axis=0, keepdims=True)
    u = d_normed * gain[...]
    back = jnp.sum(u * h, axis=-1, keepdims=True) * (root * root * root) / d
    grad_hidden[...] = upstream[...] + root * u - h * back


def whole_kernel(
    hidden, upstream, w_in, w_out, gain, taps, out_gain, skip_e, heads, meta, seq_col, seq_row,
    normed_b, mixed_b, grad_hidden, d_proj_b, g_gain, g_taps, g_out, g_heads,
    proj, act, d_act, inner, gated, stats, step, step_e, cum_e, cum_t, scores,
    d_val, d_gated, acc, d_scores,
):
    shared = (gain, taps, out_gain, skip_e, heads, meta, seq_col, seq_row)
    forward_kernel(
        hidden, w_in, *shared,
        normed_b, proj, act, d_act, inner, mixed_b, gated, stats, step, step_e, cum_e, cum_t, scores,
    )
    backward_kernel(
        hidden, upstream, w_in, w_out, *shared,
        proj, act, d_act, inner, gated, stats, step, step_e, cum_e, cum_t, scores,
        grad_hidden, d_proj_b, g_gain, g_taps, g_out, g_heads,
        d_val, d_gated, acc, d_scores,
    )


def per_device(
    hidden_in, cotangent, seq_ids, norm_gain, in_weight, conv_weight, conv_bias, out_gain,
    out_weight, decay_log, skip_gain, step_bias,
):
    n, d = hidden_in.shape
    rows, width = in_weight.shape
    padded = -(-width // LANE) * LANE
    spare = padded - width
    small = jnp.concatenate([norm_gain, conv_weight.reshape(-1), conv_bias, out_gain])
    packed = jnp.pad(small, (0, rows * spare - small.shape[0])).reshape(rows, spare)
    folds = out_weight.shape[0] // rows
    halves = [out_weight[j * rows : (j + 1) * rows] for j in range(folds)]
    sent = jnp.concatenate([in_weight, packed] + halves, axis=1)
    w_in = lax.all_gather(sent, AXES, axis=0, tiled=True)
    devices = w_in.shape[0] // rows
    w_out = jnp.stack(
        [w_in[:, padded + j * d : padded + (j + 1) * d].reshape(devices, rows, d) for j in range(folds)],
        axis=1,
    ).reshape(-1, d)
    table = w_in[:, width:padded].reshape(devices, rows * spare).astype(F32)
    sizes = [norm_gain.shape[0]] + [conv_bias.shape[0]] * (KC + 1) + [out_gain.shape[0]]
    parts, at = [], 0
    for size in sizes:
        parts.append(table[:, at : at + size].reshape(1, -1))
        at += size
    gain = parts[0]
    taps = jnp.concatenate(parts[1 : KC + 2] + [jnp.zeros((8 - KC - 1, CONV), F32)])
    o_gain = parts[KC + 2]
    skip_e = jnp.repeat(skip_gain, HD)[None]
    heads = jnp.pad(jnp.stack([step_bias, -jnp.exp(decay_log)]), ((0, 6), (0, LANE - NH)))
    matched = [
        jnp.concatenate([jnp.zeros((j,), F32), (seq_ids[j:] == seq_ids[:-j]).astype(F32)])
        for j in range(1, KC)
    ]
    meta = jnp.stack(matched + [(seq_ids >= 0).astype(F32)], axis=1)
    seq_col, seq_row = seq_ids[:, None], seq_ids[None]
    limit = pltpu.CompilerParams(vmem_limit_bytes=56 * 1024 * 1024)

    rows_first = (((0,), (0,)), ((), ()))
    normed_b, mixed_b, grad_hidden, d_proj_b, g_gain, g_taps, g_out, g_heads = pl.pallas_call(
        whole_kernel,
        name="mixer",
        out_shape=[
            sds(n, d, dtype=BF16), sds(n, DI, dtype=BF16), sds(n, d), sds(n, padded, dtype=BF16),
            sds(1, d), sds(8, CONV), sds(1, DI), sds(8, LANE),
        ],
        in_specs=[VM] * 12,
        out_specs=[VM] * 8,
        scratch_shapes=[
            pltpu.VMEM(shape, F32)
            for shape in (
                (n, padded), (n, CONV), (n, CONV), (n, DI), (n, DI), (n, LANE), (n, LANE), (n, DI),
                (n, DI), (LANE, n), (n, n), (n, CONV), (n, DI), (n, LANE), (n, n),
            )
        ],
        compiler_params=limit,
        cost_estimate=pl.CostEstimate(
            flops=12 * 10**9, bytes_accessed=10**7, transcendentals=10**6
        ),
    )(
        hidden_in, cotangent, w_in, w_out, gain, taps, o_gain, skip_e, heads, meta, seq_col, seq_row
    )
    grad_out = lax.dot_general(
        mixed_b, cotangent.astype(BF16), rows_first, preferred_element_type=F32
    ).astype(BF16)
    pieces = [g_gain] + [g_taps[j : j + 1] for j in range(KC + 1)] + [g_out]
    table = jnp.concatenate([p.reshape(devices, -1) for p in pieces], axis=1)
    table = jnp.pad(table, ((0, 0), (0, rows * spare - table.shape[1])))
    table = jnp.pad(table.reshape(devices * rows, spare), ((0, 0), (width, 0)))
    grad_in = lax.dot_general(normed_b, d_proj_b, rows_first, preferred_element_type=F32)
    split = grad_out.reshape(devices, folds, rows, d)
    partial = jnp.concatenate(
        [(grad_in + table).astype(BF16)] + [split[:, j].reshape(-1, d) for j in range(folds)], axis=1
    )
    partial, g_heads = lax.optimization_barrier((partial, g_heads))
    own = lax.psum_scatter(partial, AXES, scatter_dimension=0, tiled=True).astype(F32)
    own_out = jnp.concatenate(
        [own[:, padded + j * d : padded + (j + 1) * d] for j in range(folds)], axis=0
    )
    block_out = hidden_in + jnp.dot(mixed_b, w_out, preferred_element_type=F32)
    head_sums = lax.psum(g_heads, AXES)
    tail = own[:, width:padded].reshape(-1)
    outs, at = [], 0
    for size in sizes:
        outs.append(tail[at : at + size])
        at += size
    return (
        block_out,
        grad_hidden,
        outs[0],
        own[:, :width],
        jnp.stack(outs[1 : KC + 1]),
        outs[KC + 1],
        outs[KC + 2],
        own_out,
        head_sums[0, :NH],
        head_sums[1, :NH],
        head_sums[2, :NH],
    )


MESH = pl.DeviceIdType.MESH
LOG2E = 1.4426950408889634
GROUP = 4
WIDE = 2 * LANE
TAIL = DI + CONV + LANE
FULL = TAIL + LANE


def lanes_of(k, width):
    return lax.broadcasted_iota(jnp.int32, (1, width), 1) + k * width


def owner(lane, period):
    return jnp.floor((lane.astype(F32) + 0.5) * (1.0 / period))


def soft(x):
    return 0.5 * jnp.tanh(0.5 * x) + 0.5


def split3(x):
    a = x.astype(BF16)
    r = x - a.astype(F32)
    b = r.astype(BF16)
    return a, b, (r - b.astype(F32)).astype(BF16)


def dot3(parts, e):
    return dot(parts[0], e) + dot(parts[1], e) + dot(parts[2], e)


def fused_kernel(side, *refs):
    (
        hidden, upstream, w_own, wo_own, tile, heads, seq,
        block_out, grad_hidden, own_in, own_out, own_small, head_sums,
        wi, wo, gi, go, c0i, c1i, c2i, c3i, c0o, c1o, c2o, c3o, hz, hy, hx, hc,
        proj, act, d_act, inner, gated, d_gated, cum_w, size_e, cum_t, taps, gains, ogains,
        same, live, mk, mk_t, sm, sm_t, ds_t, nb, n_t, mixed, up_b, d_proj, d_normed,
        flow, flow_v, d_cum, d_step, size, raw, stats, scale_w, pull_w, head_e, g_taps, g_out, g_skip,
        small, lhs, send_sems, recv_sems,
    ) = refs
    nz = wi.shape[0]
    rows, rows_o = wi.shape[3] // 2, wo.shape[3] // 2
    n, d = hidden.shape
    count = nz * side * side * 2
    half_n = n // 2
    per_conv, per_in, per_out = CONV // count, d // count, DI // count
    dp, fs = lax.axis_index("dp"), lax.axis_index("fsdp")
    z, y = lax.div(dp, side), lax.rem(dp, side)
    x, c = lax.div(fs, 2), lax.rem(fs, 2)

    def at(z_, y_, x_, c_):
        return {"dp": z_ * side + y_, "fsdp": x_ * 2 + c_}

    z_peers = [lax.rem(z + j, nz) for j in range(1, nz)]
    y_peers = [lax.rem(y + j, side) for j in range(1, side)]
    x_peers = [lax.rem(x + j, side) for j in range(1, side)]
    partner = at(z, y, x, 1 - c)
    everyone = (
        [at(p, y, x, c) for p in z_peers]
        + [at(z, p, x, c) for p in y_peers]
        + [at(z, y, p, c) for p in x_peers]
        + [partner]
    )

    barrier = pltpu.get_barrier_semaphore()
    for device in everyone:
        pl.semaphore_signal(barrier, inc=1, device_id=device, device_id_type=MESH)
    width = w_own.shape[1]

    def core(ref, which):
        size_ = ref.shape[3] // 2
        return pl.ds(pl.multiple_of(which * size_, 8), size_)

    mine = core(wi, c)
    wi[z, y, x, mine, pl.ds(DI + CONV, TAIL - DI - CONV)] = jnp.zeros((rows, LANE), BF16)
    wi[z, y, x, mine, pl.ds(TAIL, LANE)] = jnp.zeros((rows, LANE), BF16)
    wi[z, y, x, mine, pl.ds(0, width)] = w_own[...]
    wi[z, y, x, pl.ds(pl.multiple_of(c * rows, 8), 8), pl.ds(TAIL, LANE)] = tile[...]
    wo[z, y, x, core(wo, c), :] = wo_own[...]
    pl.semaphore_wait(barrier, len(everyone))

    flights, state = {}, [0]

    def launch(key, moves):
        copies = []
        for src, dst, device in moves:
            i = state[0]
            state[0] += 1
            copy = pltpu.make_async_remote_copy(
                src_ref=src, dst_ref=dst, send_sem=send_sems.at[i], recv_sem=recv_sems.at[i],
                device_id=device, device_id_type=MESH,
            )
            copy.start()
            copies.append(copy)
        flights[key] = copies

    def arrive(key):
        for copy in flights[key]:
            copy.wait_recv()

    tail_at = DI + CONV - 2 * NS
    passes = [("t", wi, (pl.ds(tail_at, 2 * NS), pl.ds(tail_at + 2 * NS, WIDE)))]
    step_cols = GROUP * LANE
    groups = NH // 2 // GROUP
    for g in range(groups):
        passes.append((g, wi, (pl.ds(g * step_cols, step_cols), pl.ds(DI + g * step_cols, step_cols))))
    passes.append(("o", wo, (pl.ds(0, d // 2), pl.ds(d // 2, d // 2))))

    def gather0(p):
        name, w, halves = passes[p]
        for h, cols_h in enumerate(halves):
            ref = w.at[z, y, x, core(w, c), cols_h]
            launch(("a", name, h, 0), [(ref, ref, at(q, y, x, c)) for q in z_peers])

    def gather1(p):
        name, w, halves = passes[p]
        for h, cols_h in enumerate(halves):
            arrive(("a", name, h, 0))
            ref = w.at[:, y, x, core(w, c), cols_h]
            to = [at(z, y, q, c) for q in x_peers] if h == 0 else [at(z, q, x, c) for q in y_peers]
            launch(("a", name, h, 1), [(ref, ref, q) for q in to])

    def gather2(p):
        name, w, halves = passes[p]
        for h, cols_h in enumerate(halves):
            arrive(("a", name, h, 1))
            ref = w.at[:, y, :, core(w, c), cols_h] if h == 0 else w.at[:, :, x, core(w, c), cols_h]
            to = [at(z, q, x, c) for q in y_peers] if h == 0 else [at(z, y, q, c) for q in x_peers]
            launch(("a", name, h, 2), [(ref, ref, q) for q in to])

    def gather3(p):
        name, w, halves = passes[p]
        for h, cols_h in enumerate(halves):
            arrive(("a", name, h, 2))
            ref = w.at[:, :, :, core(w, c), cols_h]
            launch(("a", name, h, 3), [(ref, ref, partner)])

    def gathered(p):
        for h in range(2):
            arrive(("a", passes[p][0], h, 3))

    def reduce_refs(p):
        name, w, halves = passes[p]
        if name == "o":
            return name, go, (c0o, c1o, c2o, c3o), halves
        return name, gi, (c0i, c1i, c2i, c3i), halves

    def plus(a, b):
        return (a.astype(F32) + b.astype(F32)).astype(BF16)

    def reduce0(p):
        name, g, slots, halves = reduce_refs(p)
        for h, cols_h in enumerate(halves):
            launch(("r", name, h, 0), [(g.at[:, :, :, core(g, 1 - c), cols_h], slots[0].at[:, :, :, :, cols_h], partner)])

    def reduce1(p):
        name, g, slots, halves = reduce_refs(p)
        for h, cols_h in enumerate(halves):
            arrive(("r", name, h, 0))

            @pl.loop(0, nz)
            def _(i):
                for j in range(side):
                    for k in range(side):
                        g[i, j, k, core(g, c), cols_h] = plus(g[i, j, k, core(g, c), cols_h], slots[0][i, j, k, :, cols_h])

            if h == 0:
                moves = [
                    (g.at[:, q, :, core(g, c), cols_h], slots[1].at[j, :, :, :, cols_h], at(z, q, x, c))
                    for j, q in enumerate(y_peers)
                ]
            else:
                moves = [
                    (g.at[:, :, q, core(g, c), cols_h], slots[1].at[j, :, :, :, cols_h], at(z, y, q, c))
                    for j, q in enumerate(x_peers)
                ]
            launch(("r", name, h, 1), moves)

    def reduce2(p):
        name, g, slots, halves = reduce_refs(p)
        for h, cols_h in enumerate(halves):
            arrive(("r", name, h, 1))

            @pl.loop(0, nz)
            def _(i):
                for k in range(side):
                    place = (i, y, k, core(g, c)) if h == 0 else (i, k, x, core(g, c))
                    for j in range(side - 1):
                        g[(*place, cols_h)] = plus(
                            g[(*place, cols_h)], slots[1][j, i, k, :, cols_h]
                        )

            if h == 0:
                moves = [
                    (g.at[:, y, q, core(g, c), cols_h], slots[2].at[j, :, :, cols_h], at(z, y, q, c))
                    for j, q in enumerate(x_peers)
                ]
            else:
                moves = [
                    (g.at[:, q, x, core(g, c), cols_h], slots[2].at[j, :, :, cols_h], at(z, q, x, c))
                    for j, q in enumerate(y_peers)
                ]
            launch(("r", name, h, 2), moves)

    def reduce3(p):
        name, g, slots, halves = reduce_refs(p)
        for h, cols_h in enumerate(halves):
            arrive(("r", name, h, 2))

            @pl.loop(0, nz)
            def _(i):
                for j in range(side - 1):
                    g[i, y, x, core(g, c), cols_h] = plus(g[i, y, x, core(g, c), cols_h], slots[2][j, i, :, cols_h])

            launch(
                ("r", name, h, 3),
                [
                    (g.at[q, y, x, core(g, c), cols_h], slots[3].at[j, :, cols_h], at(q, y, x, c))
                    for j, q in enumerate(z_peers)
                ],
            )

    def reduce4(p):
        name, g, slots, halves = reduce_refs(p)
        for h, cols_h in enumerate(halves):
            arrive(("r", name, h, 3))
            total = g[z, y, x, core(g, c), cols_h].astype(F32)
            for j in range(nz - 1):
                total = total + slots[3][j, :, cols_h].astype(F32)
            if name == "o":
                own_out[:, cols_h] = total
            elif name == "t" and h == 1:
                own_in[:, pl.ds(DI + CONV, width - DI - CONV)] = total[:, : width - DI - CONV]
                own_small[...] = total[0:8, LANE:]
            else:
                own_in[:, cols_h] = total

    for p in range(len(passes)):
        gather0(p)

    wi2, wo2 = wi.reshape(d, FULL), wo.reshape(DI, d)
    gi2, go2 = gi.reshape(d, FULL), go.reshape(DI, d)

    seq_f = seq[...].astype(F32)
    seq_c = jnp.broadcast_to(seq_f, (LANE, n)).T
    row = lax.broadcasted_iota(jnp.int32, (n, LANE), 0)
    lane = lax.broadcasted_iota(jnp.int32, (1, LANE), 1)
    first = lane < HD
    for j in range(1, KC):
        same[j - 1] = ((pltpu.roll(seq_c, j, 0) == seq_c) & (row >= j)).astype(F32)
    live[...] = (seq_c >= 0.0).astype(F32)
    for j in range(n // LANE):
        cut = slice(j * LANE, (j + 1) * LANE)
        equal = seq_c == seq_f[:, cut]
        at_lane = lane + j * LANE
        mk[:, cut] = (equal & (row >= at_lane)).astype(F32).astype(BF16)
        mk_t[:, cut] = (equal & (row <= at_lane)).astype(F32).astype(BF16)
    up_b[...] = upstream[...].astype(BF16)
    small[...] = jnp.zeros_like(small)
    stats[...] = jnp.zeros_like(stats)
    ds_t[...] = jnp.zeros_like(ds_t)
    d_cum[...] = jnp.zeros_like(d_cum)
    d_step[...] = jnp.zeros_like(d_step)
    g_taps[...] = jnp.zeros_like(g_taps)
    g_skip[...] = jnp.zeros_like(g_skip)

    gather1(0)
    gather1(1)
    gather2(0)
    gather1(2)
    gather2(1)
    gather3(0)
    gathered(0)

    row_owner = (lax.broadcasted_iota(jnp.int32, (count * 8, 1), 0) // 8).astype(F32)
    head_row = lax.broadcasted_iota(jnp.int32, (LANE, 1), 0)

    def one_hot(k, period):
        lanes = lanes_of(k, WIDE)
        of = owner(lanes, period)
        within = lanes.astype(F32) - of * period
        e = (head_row.astype(F32) == within).astype(F32).astype(BF16)
        return e, row_owner == of

    pairs = wi.reshape(count // 2, 2 * rows, FULL)
    both = [pairs[:, j : j + 8, TAIL:FULL].astype(F32)[:, None] for j in (0, rows)]
    params = jnp.concatenate(both, axis=1).reshape(count * 8, LANE).astype(BF16)

    def unpack(dst, period):
        @pl.loop(0, dst.shape[1] // WIDE)
        def _(k):
            e, mine = one_hot(k, period)
            q = jnp.where(mine, dot(params, e), 0.0)
            dst[:, cols(k, WIDE)] = jnp.sum(q.reshape(count, 8, WIDE), axis=0)

    unpack(gains, per_in)
    unpack(taps, per_conv)
    unpack(ogains, per_out)

    h_in = hidden[...]
    root = lax.rsqrt(jnp.sum(h_in * h_in, axis=-1, keepdims=True) / d + EPS)
    gain = gains[5:6, :]
    nb[...] = (h_in * root * gain).astype(BF16)
    for j in range(d // LANE):
        n_t[j * LANE : (j + 1) * LANE, :] = nb[:, j * LANE : (j + 1) * LANE].T

    def project(start, size_):
        for j in range(0, size_, WIDE):
            w_ = min(WIDE, size_ - j)
            proj[:, start + j : start + j + w_] = dot(nb[...], wi2[:, start + j : start + j + w_])

    def conv(k):
        xk = proj[:, cols(k + DI // LANE)]
        tap = taps[:, cols(k)]
        total = tap[KC : KC + 1] + xk * tap[KC - 1 : KC]
        for j in range(1, KC):
            total = total + pltpu.roll(xk, j, 0) * same[j - 1] * tap[KC - 1 - j : KC - j]
        sg = soft(total)
        act[:, cols(k)] = total * sg
        d_act[:, cols(k)] = sg * (1.0 + total * (1.0 - sg))

    project(tail_at, TAIL - tail_at)
    conv(DI // LANE)
    conv(DI // LANE + 1)
    neg = -jnp.exp(heads[1:2])
    shifted = proj[:, DI + CONV : TAIL] + heads[0:1]
    raw[...] = shifted
    sizes = jnp.where(
        lane < NH, jnp.maximum(shifted, 0.0) + jnp.log1p(jnp.exp(-jnp.abs(shifted))), 0.0
    )
    size[...] = sizes
    rates = split3(sizes * (neg * LOG2E))
    running = dot(mk[...], rates[0]) + dot(mk[...], rates[1]) + dot(mk[...], rates[2])
    cum_t[...] = running.T
    for j, part in enumerate(split3(running)):
        lhs[0:n, j * LANE : (j + 1) * LANE] = part
    for j, part in enumerate(split3(sizes)):
        lhs[n : 2 * n, j * LANE : (j + 1) * LANE] = part
    head3 = lax.rem(lax.broadcasted_iota(jnp.int32, (3 * LANE, 1), 0), LANE)
    skip3 = split3(heads[...])

    @pl.loop(0, NH // 2)
    def _(k):
        e_full = (head3 == 2 * k + lax.shift_right_logical(lanes_of(0, WIDE), 7)).astype(F32).astype(BF16)
        cum_w[:, cols(k, WIDE)] = dot(lhs[0:n, :], e_full)
        e_half = (head3 == 2 * k + lax.shift_right_logical(lane, 6)).astype(F32).astype(BF16)
        size_e[:, cols(k)] = dot(lhs[n : 2 * n, :], e_half)
        head_e[:, cols(k)] = dot3(skip3, e_half[0:LANE])

    b_b = act[:, DI : DI + NS].astype(BF16)
    c_b = act[:, DI + NS : DI + 2 * NS].astype(BF16)
    scores = dot(c_b, b_b, ((1,), (1,))) * mk[...].astype(F32)
    sm[...] = scores
    sm_t[...] = scores.T

    def forward_group(g):
        project(g * step_cols, step_cols)
        project(DI + g * step_cols, step_cols)

        @pl.loop(g * GROUP, (g + 1) * GROUP)
        def _(k):
            conv(k)
            v = act[:, cols(k)]
            xb = (v * size_e[:, cols(k)]).astype(BF16)
            halves = []
            for h in range(2):
                cc = cum_w[:, cols(2 * k + h)]
                rr = cum_t[pl.ds(2 * k + h, 1), :]

                def mix(a, b):
                    ra, rb = slice(a * half_n, (a + 1) * half_n), slice(b * half_n, (b + 1) * half_n)
                    decay = jnp.exp2(jnp.minimum(cc[ra] - rr[:, rb], 0.0))
                    return (sm[ra, rb] * decay).astype(BF16)

                top = dot(mix(0, 0), xb[:half_n])
                low = dot(mix(1, 0), xb[:half_n]) + dot(mix(1, 1), xb[half_n:])
                halves.append(jnp.concatenate([top, low], axis=0))
            out = jnp.where(first, halves[0], halves[1])
            inner[:, cols(k)] = out
            gk = proj[:, cols(k)]
            zk = (out + head_e[2:3, cols(k)] * v) * gk * soft(gk)
            gated[:, cols(k)] = zk
            stats[...] += zk * zk

    gather1(3)
    gather2(2)
    gather3(1)
    gathered(1)
    forward_group(0)
    gather1(4)
    gather2(3)
    gather3(2)
    gathered(2)
    forward_group(1)
    gather2(4)
    gather3(3)
    gathered(3)
    forward_group(2)
    gather3(4)

    scale = lax.rsqrt(jnp.sum(stats[...], axis=-1, keepdims=True) / DI + EPS)
    scale_w[...] = jnp.broadcast_to(scale, (n, LANE))

    @pl.loop(0, NH // 2)
    def _(k):
        mk_b = (gated[:, cols(k)] * (scale_w[...] * live[...]) * ogains[6:7, cols(k)]).astype(BF16)
        mixed[:, cols(k)] = mk_b
        go2[cols(k), :] = dot(mk_b.T, up_b[...]).astype(BF16)

    reduce0(4)
    gathered(4)
    stats[...] = jnp.zeros_like(stats)

    @pl.loop(0, NH // 2)
    def _(k):
        dm = dot(up_b[...], wo2[cols(k), :], ((1,), (1,))) * live[...]
        zk = gated[:, cols(k)]
        g_out[6:7, cols(k)] = jnp.sum(dm * zk * scale_w[...], axis=0, keepdims=True)
        uk = dm * ogains[6:7, cols(k)]
        d_gated[:, cols(k)] = uk
        stats[...] += uk * zk

    pull = jnp.sum(stats[...], axis=-1, keepdims=True) * (scale * scale * scale) / DI
    pull_w[...] = jnp.broadcast_to(pull, (n, LANE))
    reduce1(4)
    for j in range(0, d, WIDE):
        block_out[:, j : j + WIDE] = hidden[:, j : j + WIDE] + dot(mixed[...], wo2[:, j : j + WIDE])

    eight = lax.broadcasted_iota(jnp.int32, (8, 1), 0)

    def pack(src, only, period, k):
        e, mine = one_hot(k, period)
        g8 = jnp.where(only, src[:, cols(k, WIDE)], 0.0)
        spread_g = jnp.broadcast_to(g8[None], (count, 8, WIDE)).reshape(count * 8, WIDE)
        small[...] += dot(jnp.where(mine, spread_g, 0.0).astype(BF16), e, ((1,), (1,)))

    @pl.loop(0, DI // WIDE)
    def _(k):
        pack(g_out, eight == 6, per_out, k)

    def conv_back(k, grad):
        xk = proj[:, cols(k + DI // LANE)]
        tap = taps[:, cols(k)]
        dt = grad * d_act[:, cols(k)]
        g_taps[pl.ds(KC, 1), cols(k)] = jnp.sum(dt, axis=0, keepdims=True)
        g_taps[pl.ds(KC - 1, 1), cols(k)] = jnp.sum(dt * xk, axis=0, keepdims=True)
        dc = dt * tap[KC - 1 : KC]
        for j in range(1, KC):
            ds_j = dt * same[j - 1]
            g_taps[pl.ds(KC - 1 - j, 1), cols(k)] = jnp.sum(ds_j * pltpu.roll(xk, j, 0), axis=0, keepdims=True)
            dc = dc + pltpu.roll(ds_j, n - j, 0) * tap[KC - 1 - j : KC - j]
        d_proj[:, cols(k + DI // LANE)] = dc.astype(BF16)

    def backward_pair(g, i):
        k = g * GROUP + i
        zk = gated[:, cols(k)]
        dz = scale_w[...] * d_gated[:, cols(k)] - zk * pull_w[...]
        gk = proj[:, cols(k)]
        sg = soft(gk)
        v = act[:, cols(k)]
        yk = inner[:, cols(k)]
        skip = head_e[2:3, cols(k)]
        d_proj[:, cols(k)] = (dz * (yk + skip * v) * sg * (1.0 + gk * (1.0 - sg))).astype(BF16)
        dy = dz * gk * sg
        se = size_e[:, cols(k)]
        xb = (v * se).astype(BF16)
        dyb = dy.astype(BF16)
        dxs, tops, lows = [], [], []
        for h in range(2):
            mine = first if h == 0 else jnp.logical_not(first)
            dyh = jnp.where(mine, dy, 0.0).astype(BF16)
            cc = cum_w[:, cols(2 * k + h)]
            rr = cum_t[pl.ds(2 * k + h, 1), :]

            def decay(a, b):
                ra, rb = slice(a * half_n, (a + 1) * half_n), slice(b * half_n, (b + 1) * half_n)
                e = jnp.exp2(jnp.minimum(rr[:, rb] - cc[ra], 0.0))
                return e, (sm_t[ra, rb] * e).astype(BF16)

            e00, m00 = decay(0, 0)
            e01, m01 = decay(0, 1)
            e11, m11 = decay(1, 1)
            top = dot(m00, dyb[:half_n]) + dot(m01, dyb[half_n:])
            low = dot(m11, dyb[half_n:])
            dxs.append(jnp.concatenate([top, low], axis=0))
            x0, x1 = xb[:half_n], xb[half_n:]
            y0, y1 = dyh[:half_n], dyh[half_n:]
            last = ((1,), (1,))
            ds_t[0:half_n, 0:half_n] += dot(x0, y0, last) * e00
            ds_t[0:half_n, half_n:n] += dot(x0, y1, last) * e01
            ds_t[half_n:n, half_n:n] += dot(x1, y1, last) * e11
        dx = jnp.where(first, dxs[0], dxs[1])
        flow[:, cols(i)] = dyb.astype(F32) * yk - xb.astype(F32) * dx
        flow_v[:, cols(i)] = dx * v
        g_skip[1:2, cols(k)] = jnp.sum(dy * v, axis=0, keepdims=True)
        conv_back(k, dx * se + skip * dy)

    def sum_heads(ref, e):
        f = ref[...]
        hi = f.astype(BF16)
        lo = (f - hi.astype(F32)).astype(BF16)
        return dot(hi, e) + dot(lo, e)

    def weight_grad(start, size_):
        for j in range(start, start + size_, WIDE):
            w_ = min(WIDE, start + size_ - j)
            gi2[:, j : j + w_] = dot(n_t[...], d_proj[:, j : j + w_]).astype(BF16)

    def back_normed(start, size_):
        return dot(d_proj[:, start : start + size_], wi2[:, start : start + size_], ((1,), (1,)))

    def backward_group(g):
        @pl.loop(0, GROUP)
        def _(i):
            backward_pair(g, i)

        weight_grad(g * step_cols, step_cols)
        weight_grad(DI + g * step_cols, step_cols)
        reduce0(1 + g)

    def after_group(g):
        of_row = lax.shift_right_logical(lax.broadcasted_iota(jnp.int32, (step_cols, 1), 0), 6)
        e = (of_row + 2 * GROUP * g == lane).astype(F32).astype(BF16)
        d_cum[...] += sum_heads(flow, e)
        d_step[...] += sum_heads(flow_v, e)
        more = back_normed(g * step_cols, step_cols) + back_normed(DI + g * step_cols, step_cols)
        d_normed[...] = more if g == 0 else d_normed[...] + more
        for j in range(step_cols // WIDE):
            pack(g_taps, eight <= KC, per_conv, g * (step_cols // WIDE) + j)

    backward_group(0)
    reduce2(4)
    after_group(0)
    reduce1(1)
    backward_group(1)
    reduce3(4)
    reduce2(1)
    after_group(1)
    reduce1(2)
    backward_group(2)
    reduce4(4)
    reduce3(1)
    reduce2(2)
    after_group(2)
    reduce1(3)

    d_rates = split3(d_cum[...])
    d_rate = dot(mk_t[...], d_rates[0]) + dot(mk_t[...], d_rates[1]) + dot(mk_t[...], d_rates[2])
    d_raw = jnp.where(lane < NH, (d_step[...] + d_rate * neg) * soft(raw[...]), 0.0)
    d_proj[:, DI + CONV : TAIL] = d_raw.astype(BF16)
    skips = jnp.zeros((8, LANE), F32)
    for k in range(NH // 2):
        of_row = lax.shift_right_logical(lax.broadcasted_iota(jnp.int32, (LANE, 1), 0), 6) + 2 * k
        e = (of_row == lane).astype(F32).astype(BF16)
        skips = skips + dot3(split3(g_skip[:, k * LANE : (k + 1) * LANE]), e)
    g_decay = jnp.sum(d_rate * size[...] * neg, axis=0, keepdims=True)
    g_step = jnp.sum(d_raw, axis=0, keepdims=True)
    hz[z] = skips + jnp.where(eight == 0, g_decay, 0.0) + jnp.where(eight == 2, g_step, 0.0)
    launch("hz", [(hz.at[z], hz.at[z], at(q, y, x, c)) for q in z_peers])

    def ordered(ref):
        total = ref[0]
        for j in range(1, ref.shape[0]):
            total = total + ref[j]
        return total

    ds_full = (ds_t[...] * mk_t[...].astype(F32)).astype(BF16)
    conv_back(DI // LANE, dot(ds_full, c_b))
    conv_back(DI // LANE + 1, dot(ds_full, b_b, ((0,), (0,))))
    pack(g_taps, eight <= KC, per_conv, DI // WIDE)
    weight_grad(tail_at, TAIL - tail_at)
    total_normed = d_normed[...] + back_normed(tail_at, TAIL - tail_at)
    h_in = hidden[...]
    root = lax.rsqrt(jnp.sum(h_in * h_in, axis=-1, keepdims=True) / d + EPS)
    gains[0:1, :] = jnp.sum(total_normed * h_in * root, axis=0, keepdims=True)
    d_normed[...] = total_normed

    @pl.loop(0, d // WIDE)
    def _(k):
        e, mine = one_hot(k, per_in)
        g8 = jnp.where(eight == 5, gains[0:1, cols(k, WIDE)], 0.0)
        spread_g = jnp.broadcast_to(g8[None], (count, 8, WIDE)).reshape(count * 8, WIDE)
        small[...] += dot(jnp.where(mine, spread_g, 0.0).astype(BF16), e, ((1,), (1,)))

    gi3 = gi.reshape(count // 2, 2 * rows, FULL)
    both = small[...].reshape(count // 2, 2, 8, LANE)
    blank = jnp.zeros((count // 2, rows - 8, LANE), F32)
    gi3[:, :, TAIL:FULL] = jnp.concatenate([both[:, 0], blank, both[:, 1], blank], axis=1).astype(BF16)
    reduce0(0)
    reduce2(3)
    reduce3(2)
    reduce4(1)
    arrive("hz")
    hy[y] = ordered(hz)
    launch("hy", [(hy.at[y], hy.at[y], at(z, q, x, c)) for q in y_peers])
    reduce1(0)

    u_in = d_normed[...] * gains[5:6, :]
    back = jnp.sum(u_in * h_in, axis=-1, keepdims=True) * (root * root * root) / d
    grad_hidden[...] = upstream[...] + root * u_in - h_in * back
    reduce3(3)
    reduce4(2)
    arrive("hy")
    hx[x] = ordered(hy)
    launch("hx", [(hx.at[x], hx.at[x], at(z, y, q, c)) for q in x_peers])
    reduce2(0)
    arrive("hx")
    hc[c] = ordered(hx)
    launch("hc", [(hc.at[c], hc.at[c], partner)])
    reduce3(0)
    reduce4(3)
    arrive("hc")
    head_sums[...] = ordered(hc)
    reduce4(0)
    for copies in flights.values():
        for copy in copies:
            copy.wait_send()


def fused_device(
    side, nz, hidden_in, cotangent, seq_ids, norm_gain, in_weight, conv_weight, conv_bias, out_gain,
    out_weight, decay_log, skip_gain, step_bias,
):
    n, d = hidden_in.shape
    rows, width = in_weight.shape
    rows_o = out_weight.shape[0]

    def line(v):
        return jnp.pad(v.reshape(-1, v.shape[-1]), ((0, 0), (0, LANE - v.shape[-1])))

    tile = jnp.concatenate(
        [line(conv_weight), line(conv_bias), line(norm_gain), line(out_gain), jnp.zeros((1, LANE), BF16)]
    )
    heads = jnp.pad(jnp.stack([step_bias, decay_log, skip_gain]), ((0, 5), (0, LANE - NH)))
    grid = (nz, side, side)
    copies = 2 * (len(range(NH // 2 // GROUP)) + 2) * 2 * (nz - 1 + 2 * (side - 1) + 1)
    copies += nz - 1 + 2 * (side - 1) + 1

    def bf(*shape):
        return pltpu.VMEM(shape, BF16)

    def fl(*shape):
        return pltpu.VMEM(shape, F32)

    scratch = [
        bf(*grid, 2 * rows, FULL), bf(*grid, 2 * rows_o, d), bf(*grid, 2 * rows, FULL), bf(*grid, 2 * rows_o, d),
        bf(*grid, rows, FULL), bf(side - 1, nz, side, rows, FULL), bf(side - 1, nz, rows, FULL), bf(nz - 1, rows, FULL),
        bf(*grid, rows_o, d), bf(side - 1, nz, side, rows_o, d), bf(side - 1, nz, rows_o, d), bf(nz - 1, rows_o, d),
        fl(nz, 8, LANE), fl(side, 8, LANE), fl(side, 8, LANE), fl(2, 8, LANE),
        fl(n, TAIL), fl(n, CONV), fl(n, CONV), fl(n, DI), fl(n, DI), fl(n, DI), fl(n, NH * LANE), fl(n, DI),
        fl(LANE, n), fl(8, CONV), fl(8, d), fl(8, DI),
        fl(KC - 1, n, LANE), fl(n, LANE), bf(n, n), bf(n, n), fl(n, n), fl(n, n), fl(n, n),
        bf(n, d), bf(d, n), bf(n, DI), bf(n, d), bf(n, TAIL), fl(n, d),
        fl(n, GROUP * LANE), fl(n, GROUP * LANE), fl(n, LANE), fl(n, LANE), fl(n, LANE), fl(n, LANE),
        fl(n, LANE), fl(n, LANE), fl(n, LANE), fl(8, DI), fl(8, CONV), fl(8, DI), fl(8, DI),
        fl(2 * nz * side * side * 8, LANE), bf(2 * n, 3 * LANE),
        pltpu.SemaphoreType.DMA((copies,)), pltpu.SemaphoreType.DMA((copies,)),
    ]

    def kernel(*refs):
        fused_kernel(side, *refs)

    block_out, grad_hidden, own_in, own_out, own_small, head_sums = pl.pallas_call(
        kernel,
        name="block",
        out_shape=[sds(n, d), sds(n, d), sds(rows, width), sds(rows_o, d), sds(8, LANE), sds(8, LANE)],
        in_specs=[VM] * 7,
        out_specs=[VM] * 6,
        scratch_shapes=scratch,
        compiler_params=pltpu.CompilerParams(
            vmem_limit_bytes=67043328, collective_id=0, has_side_effects=True
        ),
    )(hidden_in, cotangent, in_weight, out_weight, tile, heads, seq_ids[None])
    return (
        block_out,
        grad_hidden,
        own_small[KC + 1, : norm_gain.shape[0]],
        own_in,
        own_small[:KC, : conv_bias.shape[0]],
        own_small[KC, : conv_bias.shape[0]],
        own_small[KC + 2, : out_gain.shape[0]],
        own_out,
        head_sums[0, :NH],
        head_sums[1, :NH],
        head_sums[2, :NH],
    )


def solution(mesh):
    rows, flat = P(AXES, None), P(AXES)
    across, inside = mesh.shape["dp"], mesh.shape["fsdp"]
    side = inside // 2

    def per_shard(*args):
        depth, depth_o = args[4].shape[0], args[8].shape[0]
        whole = inside % 2 == 0 and side > 1 and across % side == 0 and across > side
        if whole and depth % 8 == 0 and depth_o % 8 == 0 and depth >= 8 and args[0].shape[0] == 2 * LANE:
            return fused_device(side, across // side, *args)
        return per_device(*args)

    return jax.shard_map(
        per_shard,
        mesh=mesh,
        in_specs=(rows, rows, flat, flat, rows, P(None, AXES), flat, flat, rows, P(), P(), P()),
        out_specs=(rows, rows, flat, rows, P(None, AXES), flat, flat, rows, P(), P(), P()),
        check_vma=False,
    )
```

```python
import jax
import jax.numpy as jnp
from jax import lax
from jax.experimental import pallas as pl
from jax.experimental.pallas import tpu as pltpu
from jax.sharding import PartitionSpec as P

NS = 128
HD = 64
NH = 24
KC = 4
DI = 1536
CONV = 1792
LANE = 128
EPS = 1e-05
AXES = ("dp", "fsdp")
F32 = jnp.float32
BF16 = jnp.bfloat16
HIGH = lax.Precision.HIGHEST
VM = pl.BlockSpec(memory_space=pltpu.VMEM)


def sds(*shape, dtype=F32):
    return jax.ShapeDtypeStruct(shape, dtype)


def cols(k, width=LANE):
    return pl.ds(pl.multiple_of(k * width, LANE), width)


def sigmoid(x):
    return 1.0 / (1.0 + jnp.exp(-x))


def dot(a, b, dims=((1,), (0,)), precision=None):
    return lax.dot_general(
        a, b, (dims, ((), ())), precision=precision, preferred_element_type=F32
    )


def pair_masks():
    lane = lax.broadcasted_iota(jnp.int32, (1, LANE), 1)
    first = (lane < HD).astype(F32)
    return first, 1.0 - first


def spread(width_from, k):
    head = lax.broadcasted_iota(jnp.int32, (width_from, LANE), 0)
    lane = lax.broadcasted_iota(jnp.int32, (width_from, LANE), 1)
    return (head == 2 * k + lane // HD).astype(F32)


def pair_decay(cum_e, cum_t, k, mask):
    two = cum_e[:, cols(k)]
    low = jnp.float32(-1e30)
    first = two[:, 0:1] - cum_t[pl.ds(2 * k, 1), :]
    second = two[:, HD : HD + 1] - cum_t[pl.ds(2 * k + 1, 1), :]
    return jnp.exp(jnp.where(mask, first, low)), jnp.exp(jnp.where(mask, second, low))


def same_mask(seq_col, seq_row):
    n = seq_col.shape[0]
    row = lax.broadcasted_iota(jnp.int32, (n, n), 0)
    col = lax.broadcasted_iota(jnp.int32, (n, n), 1)
    return (seq_col[...] == seq_row[...]) & (row >= col)


def forward_kernel(
    hidden, w_in, gain, taps, out_gain, skip_e, heads, meta, seq_col, seq_row,
    normed_b, proj, act, d_act, inner, mixed_b, gated, stats, step, step_e, cum_e, cum_t, scores,
):
    h = hidden[...]
    n, d = h.shape
    root = lax.rsqrt(jnp.sum(h * h, axis=-1, keepdims=True) / d + EPS)
    nb = (h * root * gain[...]).astype(BF16)
    normed_b[...] = nb
    wide = 3 * LANE

    @pl.loop(0, proj.shape[1] // wide)
    def _(k):
        proj[:, cols(k, wide)] = dot(nb, w_in[:, cols(k, wide)])

    same = [meta[:, j : j + 1] for j in range(KC - 1)]

    @pl.loop(0, CONV // LANE)
    def _(k):
        x = proj[:, cols(k + DI // LANE)]
        tap = taps[:, cols(k)]
        total = tap[KC : KC + 1] + x * tap[KC - 1 : KC]
        for j in range(1, KC):
            total = total + pltpu.roll(x, j, 0) * same[j - 1] * tap[KC - 1 - j : KC - j]
        sg = sigmoid(total)
        act[:, cols(k)] = total * sg
        d_act[:, cols(k)] = sg * (1.0 + total * (1.0 - sg))

    mask = same_mask(seq_col, seq_row)
    raw = proj[:, DI + CONV : DI + CONV + LANE] + heads[0:1]
    lane = lax.broadcasted_iota(jnp.int32, (1, LANE), 1)
    size = jnp.where(
        lane < NH, jnp.maximum(raw, 0.0) + jnp.log1p(jnp.exp(-jnp.abs(raw))), 0.0
    )
    step[...] = size
    running = dot(mask.astype(F32), size * heads[1:2], precision=HIGH)
    cum_t[...] = running.T
    b = act[:, DI : DI + NS].astype(BF16)
    c = act[:, DI + NS : DI + 2 * NS].astype(BF16)
    scores[...] = dot(c, b, ((1,), (1,)))
    first, second = pair_masks()
    stats[...] = jnp.zeros_like(stats)

    @pl.loop(0, NH // 2)
    def _(k):
        e = spread(LANE, k)
        cum_e[:, cols(k)] = dot(running, e, precision=HIGH)
        size_e = dot(size, e, precision=HIGH)
        step_e[:, cols(k)] = size_e
        decay0, decay1 = pair_decay(cum_e, cum_t, k, mask)
        v = act[:, cols(k)]
        x = v * size_e
        s = scores[...]
        y = dot((s * decay0).astype(BF16), (x * first).astype(BF16)) + dot(
            (s * decay1).astype(BF16), (x * second).astype(BF16)
        )
        inner[:, cols(k)] = y
        g = proj[:, cols(k)]
        z = (y + skip_e[:, cols(k)] * v) * g * sigmoid(g)
        gated[:, cols(k)] = z
        stats[...] += z * z

    scale = lax.rsqrt(jnp.sum(stats[...], axis=-1, keepdims=True) / DI + EPS)
    live = meta[:, KC - 1 : KC]
    stats[...] = jnp.where(lane < HD, scale, root)
    factor = scale * live

    @pl.loop(0, NH // 2)
    def _(k):
        mixed_b[:, cols(k)] = (gated[:, cols(k)] * factor * out_gain[:, cols(k)]).astype(BF16)


def backward_kernel(
    hidden, upstream, w_in, w_out, gain, taps, out_gain, skip_e, heads, meta, seq_col, seq_row,
    proj, act, d_act, inner, gated, stats, step, step_e, cum_e, cum_t, scores,
    grad_hidden, d_proj_b, g_gain, g_taps, g_out, g_heads,
    d_val, d_gated, acc, d_scores,
):
    h = hidden[...]
    n, d = h.shape
    up = upstream[...].astype(BF16)
    mask = same_mask(seq_col, seq_row)
    live = meta[:, KC - 1 : KC]
    scale = stats[:, 0:1]
    root = stats[:, HD : HD + 1]
    first, second = pair_masks()
    acc[...] = jnp.zeros_like(acc)

    @pl.loop(0, NH // 2)
    def _(k):
        dm = dot(up, w_out[cols(k), :], ((1,), (1,))) * live
        z = gated[:, cols(k)]
        g_out[:, cols(k)] = jnp.sum(dm * z * scale, axis=0, keepdims=True)
        u = dm * out_gain[:, cols(k)]
        d_gated[:, cols(k)] = u
        acc[...] += u * z

    pull = jnp.sum(acc[...], axis=-1, keepdims=True) * (scale * scale * scale) / DI
    d_scores[...] = jnp.zeros_like(d_scores)
    g_heads[...] = jnp.zeros_like(g_heads)
    tall = lax.broadcasted_iota(jnp.int32, (8, 1), 0)

    def body(k, carry):
        d_cum, d_step = carry
        e = spread(LANE, k)
        dz = scale * d_gated[:, cols(k)] - gated[:, cols(k)] * pull
        g = proj[:, cols(k)]
        sg = sigmoid(g)
        v = act[:, cols(k)]
        y = inner[:, cols(k)]
        skip = skip_e[:, cols(k)]
        d_proj_b[:, cols(k)] = (
            dz * (y + skip * v) * sg * (1.0 + g * (1.0 - sg))
        ).astype(BF16)
        dy = dz * g * sg
        size_e = step_e[:, cols(k)]
        x = (v * size_e).astype(BF16)
        dyb = dy.astype(BF16)
        dy0 = (dy * first).astype(BF16)
        dy1 = (dy * second).astype(BF16)
        decay0, decay1 = pair_decay(cum_e, cum_t, k, mask)
        s = scores[...]
        dx = dot((s * decay0).astype(BF16), dy0, ((0,), (0,))) + dot(
            (s * decay1).astype(BF16), dy1, ((0,), (0,))
        )
        d_scores[...] += dot(dy0, x, ((1,), (1,))) * decay0 + dot(dy1, x, ((1,), (1,))) * decay1
        d_val[:, cols(k)] = dx * size_e + skip * dy
        flow = dyb.astype(F32) * y - x.astype(F32) * dx
        d_cum = d_cum + dot(flow, e, ((1,), (1,)), precision=HIGH)
        d_step = d_step + dot(dx * v, e, ((1,), (1,)), precision=HIGH)
        skips = jnp.sum(dy * v, axis=0, keepdims=True)
        g_heads[...] += jnp.where(
            tall == 1, dot(jnp.broadcast_to(skips, (8, LANE)), e, ((1,), (1,)), precision=HIGH), 0.0
        )
        return d_cum, d_step

    zero = jnp.zeros((n, LANE), F32)
    d_cum, d_step = lax.fori_loop(0, NH // 2, body, (zero, zero))
    d_rate = dot(mask.astype(F32), d_cum, ((0,), (0,)), precision=HIGH)
    neg = heads[1:2]
    size = step[...]
    raw = proj[:, DI + CONV : DI + CONV + LANE] + heads[0:1]
    lane = lax.broadcasted_iota(jnp.int32, (1, LANE), 1)
    d_raw = jnp.where(lane < NH, (d_step + d_rate * neg) * sigmoid(raw), 0.0)
    d_proj_b[:, DI + CONV : DI + CONV + LANE] = d_raw.astype(BF16)
    g_decay = jnp.sum(d_rate * size * neg, axis=0, keepdims=True)
    g_step = jnp.sum(d_raw, axis=0, keepdims=True)
    g_heads[...] += jnp.where(tall == 0, g_decay, 0.0) + jnp.where(tall == 2, g_step, 0.0)

    b = act[:, DI : DI + NS].astype(BF16)
    c = act[:, DI + NS : DI + 2 * NS].astype(BF16)
    ds = d_scores[...].astype(BF16)
    d_val[:, DI : DI + NS] = dot(ds, c, ((0,), (0,)))
    d_val[:, DI + NS : DI + 2 * NS] = dot(ds, b)
    same = [meta[:, j : j + 1] for j in range(KC - 1)]

    @pl.loop(0, CONV // LANE)
    def _(k):
        x = proj[:, cols(k + DI // LANE)]
        tap = taps[:, cols(k)]
        dt = d_val[:, cols(k)] * d_act[:, cols(k)]
        g_taps[pl.ds(KC, 1), cols(k)] = jnp.sum(dt, axis=0, keepdims=True)
        g_taps[pl.ds(KC - 1, 1), cols(k)] = jnp.sum(dt * x, axis=0, keepdims=True)
        dc = dt * tap[KC - 1 : KC]
        for j in range(1, KC):
            ds_j = dt * same[j - 1]
            g_taps[pl.ds(KC - 1 - j, 1), cols(k)] = jnp.sum(
                ds_j * pltpu.roll(x, j, 0), axis=0, keepdims=True
            )
            dc = dc + pltpu.roll(ds_j, n - j, 0) * tap[KC - 1 - j : KC - j]
        d_proj_b[:, cols(k + DI // LANE)] = dc.astype(BF16)

    wide = 3 * LANE

    def add(k, total):
        return total + dot(d_proj_b[:, cols(k, wide)], w_in[:, cols(k, wide)], ((1,), (1,)))

    d_normed = lax.fori_loop(0, d_proj_b.shape[1] // wide, add, jnp.zeros((n, d), F32))
    g_gain[...] = jnp.sum(d_normed * h * root, axis=0, keepdims=True)
    u = d_normed * gain[...]
    back = jnp.sum(u * h, axis=-1, keepdims=True) * (root * root * root) / d
    grad_hidden[...] = upstream[...] + root * u - h * back


def whole_kernel(
    hidden, upstream, w_in, w_out, gain, taps, out_gain, skip_e, heads, meta, seq_col, seq_row,
    normed_b, mixed_b, grad_hidden, d_proj_b, g_gain, g_taps, g_out, g_heads,
    proj, act, d_act, inner, gated, stats, step, step_e, cum_e, cum_t, scores,
    d_val, d_gated, acc, d_scores,
):
    shared = (gain, taps, out_gain, skip_e, heads, meta, seq_col, seq_row)
    forward_kernel(
        hidden, w_in, *shared,
        normed_b, proj, act, d_act, inner, mixed_b, gated, stats, step, step_e, cum_e, cum_t, scores,
    )
    backward_kernel(
        hidden, upstream, w_in, w_out, *shared,
        proj, act, d_act, inner, gated, stats, step, step_e, cum_e, cum_t, scores,
        grad_hidden, d_proj_b, g_gain, g_taps, g_out, g_heads,
        d_val, d_gated, acc, d_scores,
    )


def per_device(
    hidden_in, cotangent, seq_ids, norm_gain, in_weight, conv_weight, conv_bias, out_gain,
    out_weight, decay_log, skip_gain, step_bias,
):
    n, d = hidden_in.shape
    rows, width = in_weight.shape
    padded = -(-width // LANE) * LANE
    spare = padded - width
    small = jnp.concatenate([norm_gain, conv_weight.reshape(-1), conv_bias, out_gain])
    packed = jnp.pad(small, (0, rows * spare - small.shape[0])).reshape(rows, spare)
    folds = out_weight.shape[0] // rows
    halves = [out_weight[j * rows : (j + 1) * rows] for j in range(folds)]
    sent = jnp.concatenate([in_weight, packed] + halves, axis=1)
    w_in = lax.all_gather(sent, AXES, axis=0, tiled=True)
    devices = w_in.shape[0] // rows
    w_out = jnp.stack(
        [w_in[:, padded + j * d : padded + (j + 1) * d].reshape(devices, rows, d) for j in range(folds)],
        axis=1,
    ).reshape(-1, d)
    table = w_in[:, width:padded].reshape(devices, rows * spare).astype(F32)
    sizes = [norm_gain.shape[0]] + [conv_bias.shape[0]] * (KC + 1) + [out_gain.shape[0]]
    parts, at = [], 0
    for size in sizes:
        parts.append(table[:, at : at + size].reshape(1, -1))
        at += size
    gain = parts[0]
    taps = jnp.concatenate(parts[1 : KC + 2] + [jnp.zeros((8 - KC - 1, CONV), F32)])
    o_gain = parts[KC + 2]
    skip_e = jnp.repeat(skip_gain, HD)[None]
    heads = jnp.pad(jnp.stack([step_bias, -jnp.exp(decay_log)]), ((0, 6), (0, LANE - NH)))
    matched = [
        jnp.concatenate([jnp.zeros((j,), F32), (seq_ids[j:] == seq_ids[:-j]).astype(F32)])
        for j in range(1, KC)
    ]
    meta = jnp.stack(matched + [(seq_ids >= 0).astype(F32)], axis=1)
    seq_col, seq_row = seq_ids[:, None], seq_ids[None]
    limit = pltpu.CompilerParams(vmem_limit_bytes=56 * 1024 * 1024)

    rows_first = (((0,), (0,)), ((), ()))
    normed_b, mixed_b, grad_hidden, d_proj_b, g_gain, g_taps, g_out, g_heads = pl.pallas_call(
        whole_kernel,
        name="mixer",
        out_shape=[
            sds(n, d, dtype=BF16), sds(n, DI, dtype=BF16), sds(n, d), sds(n, padded, dtype=BF16),
            sds(1, d), sds(8, CONV), sds(1, DI), sds(8, LANE),
        ],
        in_specs=[VM] * 12,
        out_specs=[VM] * 8,
        scratch_shapes=[
            pltpu.VMEM(shape, F32)
            for shape in (
                (n, padded), (n, CONV), (n, CONV), (n, DI), (n, DI), (n, LANE), (n, LANE), (n, DI),
                (n, DI), (LANE, n), (n, n), (n, CONV), (n, DI), (n, LANE), (n, n),
            )
        ],
        compiler_params=limit,
        cost_estimate=pl.CostEstimate(
            flops=12 * 10**9, bytes_accessed=10**7, transcendentals=10**6
        ),
    )(
        hidden_in, cotangent, w_in, w_out, gain, taps, o_gain, skip_e, heads, meta, seq_col, seq_row
    )
    grad_out = lax.dot_general(
        mixed_b, cotangent.astype(BF16), rows_first, preferred_element_type=F32
    ).astype(BF16)
    pieces = [g_gain] + [g_taps[j : j + 1] for j in range(KC + 1)] + [g_out]
    table = jnp.concatenate([p.reshape(devices, -1) for p in pieces], axis=1)
    table = jnp.pad(table, ((0, 0), (0, rows * spare - table.shape[1])))
    table = jnp.pad(table.reshape(devices * rows, spare), ((0, 0), (width, 0)))
    grad_in = lax.dot_general(normed_b, d_proj_b, rows_first, preferred_element_type=F32)
    split = grad_out.reshape(devices, folds, rows, d)
    partial = jnp.concatenate(
        [(grad_in + table).astype(BF16)] + [split[:, j].reshape(-1, d) for j in range(folds)], axis=1
    )
    partial, g_heads = lax.optimization_barrier((partial, g_heads))
    own = lax.psum_scatter(partial, AXES, scatter_dimension=0, tiled=True).astype(F32)
    own_out = jnp.concatenate(
        [own[:, padded + j * d : padded + (j + 1) * d] for j in range(folds)], axis=0
    )
    block_out = hidden_in + jnp.dot(mixed_b, w_out, preferred_element_type=F32)
    head_sums = lax.psum(g_heads, AXES)
    tail = own[:, width:padded].reshape(-1)
    outs, at = [], 0
    for size in sizes:
        outs.append(tail[at : at + size])
        at += size
    return (
        block_out,
        grad_hidden,
        outs[0],
        own[:, :width],
        jnp.stack(outs[1 : KC + 1]),
        outs[KC + 1],
        outs[KC + 2],
        own_out,
        head_sums[0, :NH],
        head_sums[1, :NH],
        head_sums[2, :NH],
    )


MESH = pl.DeviceIdType.MESH
LOG2E = 1.4426950408889634
GROUP = 2
WIDE = 2 * LANE
TAIL = DI + CONV + LANE
FULL = TAIL + LANE


def lanes_of(k, width):
    return lax.broadcasted_iota(jnp.int32, (1, width), 1) + k * width


def owner(lane, period):
    return jnp.floor((lane.astype(F32) + 0.5) * (1.0 / period))


def soft(x):
    return 0.5 * jnp.tanh(0.5 * x) + 0.5


def split3(x):
    a = x.astype(BF16)
    r = x - a.astype(F32)
    b = r.astype(BF16)
    return a, b, (r - b.astype(F32)).astype(BF16)


def dot3(parts, e):
    return dot(parts[0], e) + dot(parts[1], e) + dot(parts[2], e)


def fused_kernel(side, *refs):
    (
        hidden, upstream, w_own, wo_own, seq, conv_w, conv_b, gain_own, out_own, bias_h, decay_h, skip_h,
        block_out, grad_hidden, own_in, own_out, own_small, head_sums,
        wi, wo, gi, go, c0i, c1i, c2i, c3i, c0o, c1o, c2o, c3o, hz, hy, hx, hc,
        proj, act, d_act, inner, gated, d_gated, cum_w, size_e, cum_t, taps, gains, ogains,
        same, live, mk, mk_t, sm, sm_t, ds_t, nb, n_t, mixed, up_b, d_proj, d_normed,
        flow, flow_v, d_cum, d_step, size, raw, stats, scale_w, pull_w, head_e, g_taps, g_out, g_skip,
        small, lhs, tile, heads, send_sems, recv_sems,
    ) = refs
    nz = wi.shape[0]
    rows, rows_o = wi.shape[3] // 2, wo.shape[3] // 2
    n, d = hidden.shape
    count = nz * side * side * 2
    half_n = n // 2
    per_conv, per_in, per_out = CONV // count, d // count, DI // count
    dp, fs = lax.axis_index("dp"), lax.axis_index("fsdp")
    z, y = lax.div(dp, side), lax.rem(dp, side)
    x, c = lax.div(fs, 2), lax.rem(fs, 2)

    def at(z_, y_, x_, c_):
        return {"dp": z_ * side + y_, "fsdp": x_ * 2 + c_}

    z_peers = [lax.rem(z + j, nz) for j in range(1, nz)]
    y_peers = [lax.rem(y + j, side) for j in range(1, side)]
    x_peers = [lax.rem(x + j, side) for j in range(1, side)]
    partner = at(z, y, x, 1 - c)
    everyone = (
        [at(p, y, x, c) for p in z_peers]
        + [at(z, p, x, c) for p in y_peers]
        + [at(z, y, p, c) for p in x_peers]
        + [partner]
    )

    barrier = pltpu.get_barrier_semaphore()
    for device in everyone:
        pl.semaphore_signal(barrier, inc=1, device_id=device, device_id_type=MESH)
    width = w_own.shape[1]
    tile[...] = jnp.zeros_like(tile)
    heads[...] = jnp.zeros_like(heads)
    for at_row, part in ((0, conv_w), (KC, conv_b), (KC + 1, gain_own), (KC + 2, out_own)):
        tile[at_row : at_row + part.shape[0], 0 : part.shape[1]] = part[...].astype(F32)
    for at_row, part in enumerate((bias_h, decay_h, skip_h)):
        heads[at_row : at_row + 1, 0:NH] = part[...]

    def core(ref, which):
        size_ = ref.shape[3] // 2
        return pl.ds(pl.multiple_of(which * size_, 8), size_)

    mine = core(wi, c)
    wi[z, y, x, mine, pl.ds(DI + CONV, TAIL - DI - CONV)] = jnp.zeros((rows, LANE), BF16)
    wi[z, y, x, mine, pl.ds(TAIL, LANE)] = jnp.zeros((rows, LANE), BF16)
    wi[z, y, x, mine, pl.ds(0, width)] = w_own[...]
    wi[z, y, x, pl.ds(pl.multiple_of(c * rows, 8), 8), pl.ds(TAIL, LANE)] = tile[...].astype(BF16)
    wo[z, y, x, core(wo, c), :] = wo_own[...]
    pl.semaphore_wait(barrier, len(everyone))

    flights, state = {}, [0]

    def launch(key, moves):
        copies = []
        for src, dst, device in moves:
            i = state[0]
            state[0] += 1
            copy = pltpu.make_async_remote_copy(
                src_ref=src, dst_ref=dst, send_sem=send_sems.at[i], recv_sem=recv_sems.at[i],
                device_id=device, device_id_type=MESH,
            )
            copy.start()
            copies.append(copy)
        flights[key] = copies

    def arrive(key):
        for copy in flights[key]:
            copy.wait_recv()

    tail_at = DI + CONV - 2 * NS
    passes = [("t", wi, (pl.ds(tail_at, 2 * NS), pl.ds(tail_at + 2 * NS, WIDE)))]
    step_cols = GROUP * LANE
    groups = NH // 2 // GROUP
    for g in range(groups):
        passes.append((g, wi, (pl.ds(g * step_cols, step_cols), pl.ds(DI + g * step_cols, step_cols))))
    outs = d // WIDE
    for j in range(outs):
        passes.append((("o", j), wo, (pl.ds(j * WIDE, LANE), pl.ds(j * WIDE + LANE, LANE))))

    def gather0(p):
        name, w, halves = passes[p]
        for h, cols_h in enumerate(halves):
            ref = w.at[z, y, x, core(w, c), cols_h]
            launch(("a", name, h, 0), [(ref, ref, at(q, y, x, c)) for q in z_peers])

    def gather_own(p):
        name, w, halves = passes[p]
        for h, cols_h in enumerate(halves):
            ref = w.at[z, y, x, core(w, c), cols_h]
            to = [at(z, y, q, c) for q in x_peers] if h == 0 else [at(z, q, x, c) for q in y_peers]
            launch(("a", name, h, "own"), [(ref, ref, q) for q in to])

    def gather1(p):
        name, w, halves = passes[p]
        for h, cols_h in enumerate(halves):
            arrive(("a", name, h, 0))
            to = [at(z, y, q, c) for q in x_peers] if h == 0 else [at(z, q, x, c) for q in y_peers]
            launch(
                ("a", name, h, 1),
                [(w.at[r, y, x, core(w, c), cols_h], w.at[r, y, x, core(w, c), cols_h], q) for q in to for r in z_peers],
            )

    def gather2(p):
        name, w, halves = passes[p]
        for h, cols_h in enumerate(halves):
            arrive(("a", name, h, 1))
            arrive(("a", name, h, "own"))
            ref = w.at[:, y, :, core(w, c), cols_h] if h == 0 else w.at[:, :, x, core(w, c), cols_h]
            to = [at(z, q, x, c) for q in y_peers] if h == 0 else [at(z, y, q, c) for q in x_peers]
            launch(("a", name, h, 2), [(ref, ref, q) for q in to])

    def gather3(p):
        name, w, halves = passes[p]
        for h, cols_h in enumerate(halves):
            arrive(("a", name, h, 2))
            ref = w.at[:, :, :, core(w, c), cols_h]
            launch(("a", name, h, 3), [(ref, ref, partner)])

    def gathered(p):
        for h in range(2):
            arrive(("a", passes[p][0], h, 3))

    def reduce_refs(p):
        name, w, halves = passes[p]
        if w is wo:
            return name, go, (c0o, c1o, c2o, c3o), halves
        return name, gi, (c0i, c1i, c2i, c3i), halves

    def plus(a, b):
        return (a.astype(F32) + b.astype(F32)).astype(BF16)

    def reduce0(p):
        name, g, slots, halves = reduce_refs(p)
        for h, cols_h in enumerate(halves):
            launch(("r", name, h, 0), [(g.at[:, :, :, core(g, 1 - c), cols_h], slots[0].at[:, :, :, :, cols_h], partner)])

    def reduce1(p):
        name, g, slots, halves = reduce_refs(p)
        for h, cols_h in enumerate(halves):
            arrive(("r", name, h, 0))

            @pl.loop(0, nz)
            def _(i):
                for j in range(side):
                    for k in range(side):
                        g[i, j, k, core(g, c), cols_h] = plus(g[i, j, k, core(g, c), cols_h], slots[0][i, j, k, :, cols_h])

            if h == 0:
                moves = [
                    (g.at[:, q, :, core(g, c), cols_h], slots[1].at[j, :, :, :, cols_h], at(z, q, x, c))
                    for j, q in enumerate(y_peers)
                ]
            else:
                moves = [
                    (g.at[:, :, q, core(g, c), cols_h], slots[1].at[j, :, :, :, cols_h], at(z, y, q, c))
                    for j, q in enumerate(x_peers)
                ]
            launch(("r", name, h, 1), moves)

    def reduce2(p):
        name, g, slots, halves = reduce_refs(p)
        for h, cols_h in enumerate(halves):
            arrive(("r", name, h, 1))

            @pl.loop(0, nz)
            def _(i):
                for k in range(side):
                    place = (i, y, k, core(g, c)) if h == 0 else (i, k, x, core(g, c))
                    for j in range(side - 1):
                        g[(*place, cols_h)] = plus(
                            g[(*place, cols_h)], slots[1][j, i, k, :, cols_h]
                        )

            if h == 0:
                moves = [
                    (g.at[:, y, q, core(g, c), cols_h], slots[2].at[j, :, :, cols_h], at(z, y, q, c))
                    for j, q in enumerate(x_peers)
                ]
            else:
                moves = [
                    (g.at[:, q, x, core(g, c), cols_h], slots[2].at[j, :, :, cols_h], at(z, q, x, c))
                    for j, q in enumerate(y_peers)
                ]
            launch(("r", name, h, 2), moves)

    def reduce3(p):
        name, g, slots, halves = reduce_refs(p)
        for h, cols_h in enumerate(halves):
            arrive(("r", name, h, 2))

            @pl.loop(0, nz)
            def _(i):
                for j in range(side - 1):
                    g[i, y, x, core(g, c), cols_h] = plus(g[i, y, x, core(g, c), cols_h], slots[2][j, i, :, cols_h])

            launch(
                ("r", name, h, 3),
                [
                    (g.at[q, y, x, core(g, c), cols_h], slots[3].at[j, :, cols_h], at(q, y, x, c))
                    for j, q in enumerate(z_peers)
                ],
            )

    def reduce4(p):
        name, g, slots, halves = reduce_refs(p)
        for h, cols_h in enumerate(halves):
            arrive(("r", name, h, 3))
            total = g[z, y, x, core(g, c), cols_h].astype(F32)
            for j in range(nz - 1):
                total = total + slots[3][j, :, cols_h].astype(F32)
            if g is go:
                own_out[:, cols_h] = total
            elif name == "t" and h == 1:
                own_in[:, pl.ds(DI + CONV, width - DI - CONV)] = total[:, : width - DI - CONV]
                own_small[...] = total[0:8, LANE:]
            else:
                own_in[:, cols_h] = total

    def gather_tick(t):
        for stage, step in enumerate((gather1, gather2, gather3, gathered)):
            if 0 <= t - stage < len(passes):
                step(t - stage)

    order = [1 + groups + j for j in range(outs)] + [1 + g for g in range(groups)] + [0]

    def reduce_tick(t):
        for stage, step in enumerate((reduce0, reduce1, reduce2, reduce3, reduce4)):
            if 0 <= t - stage < len(order):
                step(order[t - stage])

    for p in range(len(passes)):
        gather_own(p)
        gather0(p)

    wi2, wo2 = wi.reshape(d, FULL), wo.reshape(DI, d)
    gi2, go2 = gi.reshape(d, FULL), go.reshape(DI, d)

    seq_f = seq[...].astype(F32)
    seq_c = jnp.broadcast_to(seq_f, (LANE, n)).T
    row = lax.broadcasted_iota(jnp.int32, (n, LANE), 0)
    lane = lax.broadcasted_iota(jnp.int32, (1, LANE), 1)
    first = lane < HD
    for j in range(1, KC):
        same[j - 1] = ((pltpu.roll(seq_c, j, 0) == seq_c) & (row >= j)).astype(F32)
    live[...] = (seq_c >= 0.0).astype(F32)
    for j in range(n // LANE):
        cut = slice(j * LANE, (j + 1) * LANE)
        equal = seq_c == seq_f[:, cut]
        at_lane = lane + j * LANE
        mk[:, cut] = (equal & (row >= at_lane)).astype(F32).astype(BF16)
        mk_t[:, cut] = (equal & (row <= at_lane)).astype(F32).astype(BF16)
    up_b[...] = upstream[...].astype(BF16)
    small[...] = jnp.zeros_like(small)
    stats[...] = jnp.zeros_like(stats)
    ds_t[...] = jnp.zeros_like(ds_t)
    d_cum[...] = jnp.zeros_like(d_cum)
    d_step[...] = jnp.zeros_like(d_step)
    g_taps[...] = jnp.zeros_like(g_taps)
    g_skip[...] = jnp.zeros_like(g_skip)

    for t in range(4):
        gather_tick(t)

    row_owner = (lax.broadcasted_iota(jnp.int32, (count * 8, 1), 0) // 8).astype(F32)
    head_row = lax.broadcasted_iota(jnp.int32, (LANE, 1), 0)

    def one_hot(k, period):
        lanes = lanes_of(k, WIDE)
        of = owner(lanes, period)
        within = lanes.astype(F32) - of * period
        e = (head_row.astype(F32) == within).astype(F32).astype(BF16)
        return e, row_owner == of

    pairs = wi.reshape(count // 2, 2 * rows, FULL)
    both = [pairs[:, j : j + 8, TAIL:FULL].astype(F32)[:, None] for j in (0, rows)]
    params = jnp.concatenate(both, axis=1).reshape(count * 8, LANE).astype(BF16)

    def unpack(dst, period):
        @pl.loop(0, dst.shape[1] // WIDE)
        def _(k):
            e, mine = one_hot(k, period)
            q = jnp.where(mine, dot(params, e), 0.0)
            dst[:, cols(k, WIDE)] = jnp.sum(q.reshape(count, 8, WIDE), axis=0)

    unpack(gains, per_in)

    h_in = hidden[...]
    root = lax.rsqrt(jnp.sum(h_in * h_in, axis=-1, keepdims=True) / d + EPS)
    gain = gains[5:6, :]
    nb[...] = (h_in * root * gain).astype(BF16)
    for j in range(d // LANE):
        n_t[j * LANE : (j + 1) * LANE, :] = nb[:, j * LANE : (j + 1) * LANE].T

    def project(start, size_):
        for j in range(0, size_, WIDE):
            w_ = min(WIDE, size_ - j)
            proj[:, start + j : start + j + w_] = dot(nb[...], wi2[:, start + j : start + j + w_])

    def conv(k):
        xk = proj[:, cols(k + DI // LANE)]
        tap = taps[:, cols(k)]
        total = tap[KC : KC + 1] + xk * tap[KC - 1 : KC]
        for j in range(1, KC):
            total = total + pltpu.roll(xk, j, 0) * same[j - 1] * tap[KC - 1 - j : KC - j]
        sg = soft(total)
        act[:, cols(k)] = total * sg
        d_act[:, cols(k)] = sg * (1.0 + total * (1.0 - sg))

    gather_tick(4)
    unpack(taps, per_conv)
    project(tail_at, TAIL - tail_at)
    conv(DI // LANE)
    conv(DI // LANE + 1)
    neg = -jnp.exp(heads[1:2])
    shifted = proj[:, DI + CONV : TAIL] + heads[0:1]
    raw[...] = shifted
    sizes = jnp.where(
        lane < NH, jnp.maximum(shifted, 0.0) + jnp.log1p(jnp.exp(-jnp.abs(shifted))), 0.0
    )
    size[...] = sizes
    rates = split3(sizes * (neg * LOG2E))
    running = dot(mk[...], rates[0]) + dot(mk[...], rates[1]) + dot(mk[...], rates[2])
    cum_t[...] = running.T
    for j, part in enumerate(split3(running)):
        lhs[0:n, j * LANE : (j + 1) * LANE] = part
    for j, part in enumerate(split3(sizes)):
        lhs[n : 2 * n, j * LANE : (j + 1) * LANE] = part
    gather_tick(5)
    head3 = lax.rem(lax.broadcasted_iota(jnp.int32, (3 * LANE, 1), 0), LANE)
    skip3 = split3(heads[...])

    @pl.loop(0, NH // 2)
    def _(k):
        e_full = (head3 == 2 * k + lax.shift_right_logical(lanes_of(0, WIDE), 7)).astype(F32).astype(BF16)
        cum_w[:, cols(k, WIDE)] = dot(lhs[0:n, :], e_full)
        e_half = (head3 == 2 * k + lax.shift_right_logical(lane, 6)).astype(F32).astype(BF16)
        size_e[:, cols(k)] = dot(lhs[n : 2 * n, :], e_half)
        head_e[:, cols(k)] = dot3(skip3, e_half[0:LANE])

    b_b = act[:, DI : DI + NS].astype(BF16)
    c_b = act[:, DI + NS : DI + 2 * NS].astype(BF16)
    scores = dot(c_b, b_b, ((1,), (1,))) * mk[...].astype(F32)
    sm[...] = scores
    sm_t[...] = scores.T

    def forward_group(g):
        project(g * step_cols, step_cols)
        project(DI + g * step_cols, step_cols)

        @pl.loop(g * GROUP, (g + 1) * GROUP)
        def _(k):
            conv(k)
            v = act[:, cols(k)]
            xb = (v * size_e[:, cols(k)]).astype(BF16)
            halves = []
            for h in range(2):
                cc = cum_w[:, cols(2 * k + h)]
                rr = cum_t[pl.ds(2 * k + h, 1), :]

                def mix(a, b):
                    ra, rb = slice(a * half_n, (a + 1) * half_n), slice(b * half_n, (b + 1) * half_n)
                    decay = jnp.exp2(jnp.minimum(cc[ra] - rr[:, rb], 0.0))
                    return (sm[ra, rb] * decay).astype(BF16)

                top = dot(mix(0, 0), xb[:half_n])
                low = dot(mix(1, 0), xb[:half_n]) + dot(mix(1, 1), xb[half_n:])
                halves.append(jnp.concatenate([top, low], axis=0))
            out = jnp.where(first, halves[0], halves[1])
            inner[:, cols(k)] = out
            gk = proj[:, cols(k)]
            zk = (out + head_e[2:3, cols(k)] * v) * gk * soft(gk)
            gated[:, cols(k)] = zk
            stats[...] += zk * zk

    gather_tick(6)
    forward_group(0)
    gather_tick(7)
    forward_group(1)
    forward_group(2)
    for g in range(3, groups):
        gather_tick(5 + g)
        forward_group(g)
        if g == 3:
            unpack(ogains, per_out)
    for t in range(5 + groups, 1 + groups + outs + 1):
        gather_tick(t)

    scale = lax.rsqrt(jnp.sum(stats[...], axis=-1, keepdims=True) / DI + EPS)
    scale_w[...] = jnp.broadcast_to(scale, (n, LANE))

    @pl.loop(0, NH // 2)
    def _(k):
        mk_b = (gated[:, cols(k)] * (scale_w[...] * live[...]) * ogains[6:7, cols(k)]).astype(BF16)
        mixed[:, cols(k)] = mk_b
        go2[cols(k), :] = dot(mk_b.T, up_b[...]).astype(BF16)

    reduce_tick(0)
    for t in range(outs):
        gather_tick(groups + outs + 2 + t)
        if t:
            reduce_tick(t)
    stats[...] = jnp.zeros_like(stats)

    @pl.loop(0, NH // 2)
    def _(k):
        dm = dot(up_b[...], wo2[cols(k), :], ((1,), (1,))) * live[...]
        zk = gated[:, cols(k)]
        g_out[6:7, cols(k)] = jnp.sum(dm * zk * scale_w[...], axis=0, keepdims=True)
        uk = dm * ogains[6:7, cols(k)]
        d_gated[:, cols(k)] = uk
        stats[...] += uk * zk

    pull = jnp.sum(stats[...], axis=-1, keepdims=True) * (scale * scale * scale) / DI
    pull_w[...] = jnp.broadcast_to(pull, (n, LANE))
    eight = lax.broadcasted_iota(jnp.int32, (8, 1), 0)

    def pack(src, only, period, k):
        e, mine = one_hot(k, period)
        g8 = jnp.where(only, src[:, cols(k, WIDE)], 0.0)
        spread_g = jnp.broadcast_to(g8[None], (count, 8, WIDE)).reshape(count * 8, WIDE)
        small[...] += dot(jnp.where(mine, spread_g, 0.0).astype(BF16), e, ((1,), (1,)))

    def conv_back(k, grad):
        xk = proj[:, cols(k + DI // LANE)]
        tap = taps[:, cols(k)]
        dt = grad * d_act[:, cols(k)]
        g_taps[pl.ds(KC, 1), cols(k)] = jnp.sum(dt, axis=0, keepdims=True)
        g_taps[pl.ds(KC - 1, 1), cols(k)] = jnp.sum(dt * xk, axis=0, keepdims=True)
        dc = dt * tap[KC - 1 : KC]
        for j in range(1, KC):
            ds_j = dt * same[j - 1]
            g_taps[pl.ds(KC - 1 - j, 1), cols(k)] = jnp.sum(ds_j * pltpu.roll(xk, j, 0), axis=0, keepdims=True)
            dc = dc + pltpu.roll(ds_j, n - j, 0) * tap[KC - 1 - j : KC - j]
        d_proj[:, cols(k + DI // LANE)] = dc.astype(BF16)

    def backward_pair(g, i):
        k = g * GROUP + i
        zk = gated[:, cols(k)]
        dz = scale_w[...] * d_gated[:, cols(k)] - zk * pull_w[...]
        gk = proj[:, cols(k)]
        sg = soft(gk)
        v = act[:, cols(k)]
        yk = inner[:, cols(k)]
        skip = head_e[2:3, cols(k)]
        d_proj[:, cols(k)] = (dz * (yk + skip * v) * sg * (1.0 + gk * (1.0 - sg))).astype(BF16)
        dy = dz * gk * sg
        se = size_e[:, cols(k)]
        xb = (v * se).astype(BF16)
        dyb = dy.astype(BF16)
        dxs, tops, lows = [], [], []
        for h in range(2):
            mine = first if h == 0 else jnp.logical_not(first)
            dyh = jnp.where(mine, dy, 0.0).astype(BF16)
            cc = cum_w[:, cols(2 * k + h)]
            rr = cum_t[pl.ds(2 * k + h, 1), :]

            def decay(a, b):
                ra, rb = slice(a * half_n, (a + 1) * half_n), slice(b * half_n, (b + 1) * half_n)
                e = jnp.exp2(jnp.minimum(rr[:, rb] - cc[ra], 0.0))
                return e, (sm_t[ra, rb] * e).astype(BF16)

            e00, m00 = decay(0, 0)
            e01, m01 = decay(0, 1)
            e11, m11 = decay(1, 1)
            top = dot(m00, dyb[:half_n]) + dot(m01, dyb[half_n:])
            low = dot(m11, dyb[half_n:])
            dxs.append(jnp.concatenate([top, low], axis=0))
            x0, x1 = xb[:half_n], xb[half_n:]
            y0, y1 = dyh[:half_n], dyh[half_n:]
            last = ((1,), (1,))
            ds_t[0:half_n, 0:half_n] += dot(x0, y0, last) * e00
            ds_t[0:half_n, half_n:n] += dot(x0, y1, last) * e01
            ds_t[half_n:n, half_n:n] += dot(x1, y1, last) * e11
        dx = jnp.where(first, dxs[0], dxs[1])
        flow[:, cols(i)] = dyb.astype(F32) * yk - xb.astype(F32) * dx
        flow_v[:, cols(i)] = dx * v
        g_skip[1:2, cols(k)] = jnp.sum(dy * v, axis=0, keepdims=True)
        conv_back(k, dx * se + skip * dy)

    def sum_heads(ref, e):
        f = ref[...]
        hi = f.astype(BF16)
        lo = (f - hi.astype(F32)).astype(BF16)
        return dot(hi, e) + dot(lo, e)

    def weight_grad(start, size_):
        for j in range(start, start + size_, WIDE):
            w_ = min(WIDE, start + size_ - j)
            gi2[:, j : j + w_] = dot(n_t[...], d_proj[:, j : j + w_]).astype(BF16)

    def back_normed(start, size_):
        return dot(d_proj[:, start : start + size_], wi2[:, start : start + size_], ((1,), (1,)))

    def backward_group(g):
        @pl.loop(0, GROUP)
        def _(i):
            backward_pair(g, i)

        weight_grad(g * step_cols, step_cols)
        weight_grad(DI + g * step_cols, step_cols)
        reduce_tick(outs + g)

    def after_group(g):
        of_row = lax.shift_right_logical(lax.broadcasted_iota(jnp.int32, (step_cols, 1), 0), 6)
        e = (of_row + 2 * GROUP * g == lane).astype(F32).astype(BF16)
        d_cum[...] += sum_heads(flow, e)
        d_step[...] += sum_heads(flow_v, e)
        more = back_normed(g * step_cols, step_cols) + back_normed(DI + g * step_cols, step_cols)
        d_normed[...] = more if g == 0 else d_normed[...] + more
        for j in range(step_cols // WIDE):
            pack(g_taps, eight <= KC, per_conv, g * (step_cols // WIDE) + j)

    for g in range(groups):
        backward_group(g)
        after_group(g)
        if g == 0:

            @pl.loop(0, DI // WIDE)
            def _(k):
                pack(g_out, eight == 6, per_out, k)

    d_rates = split3(d_cum[...])
    d_rate = dot(mk_t[...], d_rates[0]) + dot(mk_t[...], d_rates[1]) + dot(mk_t[...], d_rates[2])
    d_raw = jnp.where(lane < NH, (d_step[...] + d_rate * neg) * soft(raw[...]), 0.0)
    d_proj[:, DI + CONV : TAIL] = d_raw.astype(BF16)
    skips = jnp.zeros((8, LANE), F32)
    for k in range(NH // 2):
        of_row = lax.shift_right_logical(lax.broadcasted_iota(jnp.int32, (LANE, 1), 0), 6) + 2 * k
        e = (of_row == lane).astype(F32).astype(BF16)
        skips = skips + dot3(split3(g_skip[:, k * LANE : (k + 1) * LANE]), e)
    g_decay = jnp.sum(d_rate * size[...] * neg, axis=0, keepdims=True)
    g_step = jnp.sum(d_raw, axis=0, keepdims=True)
    hz[z] = skips + jnp.where(eight == 0, g_decay, 0.0) + jnp.where(eight == 2, g_step, 0.0)
    launch("hz", [(hz.at[z], hz.at[z], at(q, y, x, c)) for q in z_peers])

    def ordered(ref):
        total = ref[0]
        for j in range(1, ref.shape[0]):
            total = total + ref[j]
        return total

    ds_full = (ds_t[...] * mk_t[...].astype(F32)).astype(BF16)
    conv_back(DI // LANE, dot(ds_full, c_b))
    conv_back(DI // LANE + 1, dot(ds_full, b_b, ((0,), (0,))))
    pack(g_taps, eight <= KC, per_conv, DI // WIDE)
    weight_grad(tail_at, TAIL - tail_at)
    total_normed = d_normed[...] + back_normed(tail_at, TAIL - tail_at)
    h_in = hidden[...]
    root = lax.rsqrt(jnp.sum(h_in * h_in, axis=-1, keepdims=True) / d + EPS)
    gains[0:1, :] = jnp.sum(total_normed * h_in * root, axis=0, keepdims=True)
    d_normed[...] = total_normed

    @pl.loop(0, d // WIDE)
    def _(k):
        e, mine = one_hot(k, per_in)
        g8 = jnp.where(eight == 5, gains[0:1, cols(k, WIDE)], 0.0)
        spread_g = jnp.broadcast_to(g8[None], (count, 8, WIDE)).reshape(count * 8, WIDE)
        small[...] += dot(jnp.where(mine, spread_g, 0.0).astype(BF16), e, ((1,), (1,)))

    gi3 = gi.reshape(count // 2, 2 * rows, FULL)
    both = small[...].reshape(count // 2, 2, 8, LANE)
    blank = jnp.zeros((count // 2, rows - 8, LANE), F32)
    gi3[:, :, TAIL:FULL] = jnp.concatenate([both[:, 0], blank, both[:, 1], blank], axis=1).astype(BF16)
    last = outs + groups
    reduce_tick(last)
    u_in = d_normed[...] * gains[5:6, :]
    back = jnp.sum(u_in * h_in, axis=-1, keepdims=True) * (root * root * root) / d
    grad_hidden[...] = upstream[...] + root * u_in - h_in * back
    arrive("hz")
    hy[y] = ordered(hz)
    launch("hy", [(hy.at[y], hy.at[y], at(z, q, x, c)) for q in y_peers])
    reduce_tick(last + 1)
    for j in range(0, d, WIDE):
        block_out[:, j : j + WIDE] = hidden[:, j : j + WIDE] + dot(mixed[...], wo2[:, j : j + WIDE])
    arrive("hy")
    hx[x] = ordered(hy)
    launch("hx", [(hx.at[x], hx.at[x], at(z, y, q, c)) for q in x_peers])
    reduce_tick(last + 2)
    arrive("hx")
    hc[c] = ordered(hx)
    launch("hc", [(hc.at[c], hc.at[c], partner)])
    reduce_tick(last + 3)
    arrive("hc")
    head_sums[...] = ordered(hc)
    reduce_tick(last + 4)
    for copies in flights.values():
        for copy in copies:
            copy.wait_send()


def finish_kernel(*refs):
    large, (small, heads), outs, lines = refs[0:4], refs[4:6], refs[6:10], refs[10:17]
    held, in_sems, out_sems = refs[17:21], refs[21], refs[22]
    ins = [pltpu.make_async_copy(large[i], held[i], in_sems.at[i]) for i in range(4)]
    for copy in ins:
        copy.start()
    rows = ((KC + 1, 1), (0, KC), (KC, 1), (KC + 2, 1))
    for (row, tall), line in zip(rows, lines[0:4]):
        line[...] = small[row : row + tall, 0 : line.shape[1]]
    for row, line in enumerate(lines[4:7]):
        line[...] = heads[row : row + 1, 0 : line.shape[1]]
    puts = [pltpu.make_async_copy(held[i], outs[i], out_sems.at[i]) for i in range(4)]
    for get, put in zip(ins, puts):
        get.wait()
        put.start()
    for put in puts:
        put.wait()


def fused_device(
    side, nz, hidden_in, cotangent, seq_ids, norm_gain, in_weight, conv_weight, conv_bias, out_gain,
    out_weight, decay_log, skip_gain, step_bias,
):
    n, d = hidden_in.shape
    rows, width = in_weight.shape
    rows_o = out_weight.shape[0]

    grid = (nz, side, side)
    copies = 2 * (NH // 2 // GROUP + 1 + d // WIDE) * 2 * (nz - 1 + 2 * (side - 1) + 1)
    copies += 2 * (NH // 2 // GROUP + 1 + d // WIDE) * (nz - 1) * (side - 1)
    copies += nz - 1 + 2 * (side - 1) + 1

    def bf(*shape):
        return pltpu.VMEM(shape, BF16)

    def fl(*shape):
        return pltpu.VMEM(shape, F32)

    scratch = [
        bf(*grid, 2 * rows, FULL), bf(*grid, 2 * rows_o, d), bf(*grid, 2 * rows, FULL), bf(*grid, 2 * rows_o, d),
        bf(*grid, rows, FULL), bf(side - 1, nz, side, rows, FULL), bf(side - 1, nz, rows, FULL), bf(nz - 1, rows, FULL),
        bf(*grid, rows_o, d), bf(side - 1, nz, side, rows_o, d), bf(side - 1, nz, rows_o, d), bf(nz - 1, rows_o, d),
        fl(nz, 8, LANE), fl(side, 8, LANE), fl(side, 8, LANE), fl(2, 8, LANE),
        fl(n, TAIL), fl(n, CONV), fl(n, CONV), fl(n, DI), fl(n, DI), fl(n, DI), fl(n, NH * LANE), fl(n, DI),
        fl(LANE, n), fl(8, CONV), fl(8, d), fl(8, DI),
        fl(KC - 1, n, LANE), fl(n, LANE), bf(n, n), bf(n, n), fl(n, n), fl(n, n), fl(n, n),
        bf(n, d), bf(d, n), bf(n, DI), bf(n, d), bf(n, TAIL), fl(n, d),
        fl(n, GROUP * LANE), fl(n, GROUP * LANE), fl(n, LANE), fl(n, LANE), fl(n, LANE), fl(n, LANE),
        fl(n, LANE), fl(n, LANE), fl(n, LANE), fl(8, DI), fl(8, CONV), fl(8, DI), fl(8, DI),
        fl(2 * nz * side * side * 8, LANE), bf(2 * n, 3 * LANE), fl(8, LANE), fl(8, LANE),
        pltpu.SemaphoreType.DMA((copies,)), pltpu.SemaphoreType.DMA((copies,)),
    ]

    def kernel(*refs):
        fused_kernel(side, *refs)

    block_out, grad_hidden, own_in, own_out, own_small, head_sums = pl.pallas_call(
        kernel,
        name="block",
        out_shape=[sds(n, d), sds(n, d), sds(rows, width), sds(rows_o, d), sds(8, LANE), sds(8, LANE)],
        in_specs=[VM] * 12,
        out_specs=[VM] * 6,
        scratch_shapes=scratch,
        compiler_params=pltpu.CompilerParams(
            vmem_limit_bytes=67043328, collective_id=0, has_side_effects=True
        ),
    )(
        hidden_in, cotangent, in_weight, out_weight, seq_ids[None], conv_weight, conv_bias[None],
        norm_gain[None], out_gain[None], step_bias[None], decay_log[None], skip_gain[None],
    )
    large = (block_out, grad_hidden, own_in, own_out)
    per_in, per_conv, per_out = norm_gain.shape[0], conv_bias.shape[0], out_gain.shape[0]
    lines = [sds(1, per_in), sds(KC, per_conv), sds(1, per_conv), sds(1, per_out)] + [sds(1, NH)] * 3
    anywhere = pl.BlockSpec(memory_space=pl.ANY)
    (
        block_out, grad_hidden, own_in, own_out, g_gain, g_taps, g_shift, g_out, g_decay, g_skip, g_step,
    ) = pl.pallas_call(
        finish_kernel,
        name="finish",
        out_shape=[sds(*v.shape) for v in large] + lines,
        in_specs=[anywhere] * 4 + [VM] * 2,
        out_specs=[anywhere] * 4 + [VM] * 7,
        scratch_shapes=[fl(*v.shape) for v in large]
        + [pltpu.SemaphoreType.DMA((4,)), pltpu.SemaphoreType.DMA((4,))],
    )(*large, own_small, head_sums)
    return (
        block_out, grad_hidden, g_gain[0], own_in, g_taps, g_shift[0], g_out[0], own_out,
        g_decay[0], g_skip[0], g_step[0],
    )


def solution(mesh):
    rows, flat = P(AXES, None), P(AXES)
    across, inside = mesh.shape["dp"], mesh.shape["fsdp"]
    side = inside // 2

    def per_shard(*args):
        depth, depth_o = args[4].shape[0], args[8].shape[0]
        whole = inside % 2 == 0 and side > 1 and across % side == 0 and across > side
        if whole and depth % 8 == 0 and depth_o % 8 == 0 and depth >= 8 and args[0].shape[0] == 2 * LANE:
            return fused_device(side, across // side, *args)
        return per_device(*args)

    return jax.shard_map(
        per_shard,
        mesh=mesh,
        in_specs=(rows, rows, flat, flat, rows, P(None, AXES), flat, flat, rows, P(), P(), P()),
        out_specs=(rows, rows, flat, rows, P(None, AXES), flat, flat, rows, P(), P(), P()),
        check_vma=False,
    )
```
